512 devices in a mesh: head: 4 (over x), blk: 128 (over y, z, core).
Axes of the slice: x: 4, y: 8, z: 8, core: 2. Of those that a mesh axis runs over, the one named last changes fastest.
Arguments:
- tokens: bfloat16 [8192, 2048], P('blk'), may hold values from -6 to 6
- q_weight: bfloat16 [2048, 1024], P(None, 'head')
- k_weight: bfloat16 [2048, 256], P(None, 'head')
- v_weight: bfloat16 [2048, 256], P(None, 'head'), may hold values from -0.125 to 0.125
- o_weight: bfloat16 [1024, 2048], P('head'), may hold values from -0.1875 to 0.1875
- kv_pages: bfloat16 [4, 384, 64, 128], P('head', 'blk')
- page_node: int32 [384], replicated, may hold values from 0 to 72, as said below
- page_fill: int32 [384], replicated, may hold values from 1 to 64
- req_len: int32 [64], replicated, may hold values from 1 to 256, 8192 in all
- req_leaf: int32 [64], replicated, may hold values from 0 to 63
- leaf_parent: int32 [64], replicated, may hold values from 0 to 7
Outputs:
- attn_out: bfloat16 [8192, 2048], P('blk', 'head')
The draws below stay inside these ranges and needn't reach their ends.
Inputs may be any that keep to these rules, and one draw needn't show every extreme that they name: `req_len`: their sum is 8192, and the longest request has exactly 256 tokens. `page_node`: node 0 is the root, nodes 1 to 8 form the middle level and the rest are leaves; the root holds a third of the 384 pages, each middle node a 1 / 8 share of another third, each leaf two pages, placed over the pages in any order.
All inputs are finite; a program needn't handle non-finite values.
Results may differ from the reference program's by a relative error of at most 0.012.
The reference program's roundings to bfloat16 on the way (of `normed`, `queries`, `keys_new`, `values_new`, `weights` and `attended`) count: a program that leaves them out, or rounds other values in their place, can miss the bound.
Values may be sent and summed in bfloat16 or wider, within the bound.
A program may use at most 128 MiB of HBM per device.

```python
import math
import jax
import jax.numpy as jnp
import numpy as np
from jax import lax

D = 2048
HD = 64
QH = 16
KVH = 4
PAGE = 64
MIDS = 8
PROMPT = 256
TOKENS = 8192
REQS = 64
LEAVES = 64
PAGES = 384


def draw_q_weight(key, part):
    shape = (D, QH * HD)
    base = jax.random.truncated_normal(key, -6.0, 6.0, shape, jnp.float32) * D ** (-0.5)
    return base.astype(jnp.bfloat16)


def draw_k_weight(key, part):
    shape = (D, KVH * HD)
    boost = 24.0 / math.sqrt(HD)
    base = jax.random.truncated_normal(key, -6.0, 6.0, shape, jnp.float32)
    return (base * D ** (-0.5) * boost).astype(jnp.bfloat16)


def draw_kv_pages(key, part):
    shape = (KVH, PAGES, PAGE, 2 * HD)
    key_part = jnp.arange(2 * HD) < HD
    level = 4.0 / math.sqrt(HD)
    values = jax.random.truncated_normal(key, -6.0, 6.0, shape, jnp.float32)
    page_scale = jnp.exp(jax.random.uniform(jax.random.fold_in(key, 3), (KVH, PAGES, 1, 1), jnp.float32, 0.0, math.log(4.0))) * level
    values = jnp.where(key_part, values * page_scale, values)
    return values.astype(jnp.bfloat16)


def draw_page_node(key, part):
    level_pages = PAGES // 3
    mid_pages = level_pages // MIDS
    slots = jnp.arange(PAGES, dtype=jnp.int32)
    middle = 1 + (slots - level_pages) // mid_pages
    leaves = 1 + MIDS + (slots - 2 * level_pages) // 2
    node_ids = jnp.where(slots < level_pages, 0, jnp.where(slots < 2 * level_pages, middle, leaves))
    order = jax.random.permutation(key, PAGES)
    return node_ids[order].astype(jnp.int32)


def with_ends(drawn, stream_key, low, largest):
    longest = drawn.shape.index(max(drawn.shape))
    spots = []
    for shift in (0, 1):
        where = [jax.random.randint(jax.random.fold_in(stream_key, axis), (), 0, length) for axis, length in enumerate(drawn.shape)]
        where[longest] = (where[longest] + shift) % drawn.shape[longest]
        spots.append(tuple(where))
    return drawn.at[spots[0]].set(low).at[spots[1]].set(largest)


def block_levels(stream_key, dims, pieces, low, largest):
    gain = 1.0
    for axis_at, shards_of in pieces:
        steps = jax.random.uniform(jax.random.fold_in(jax.random.fold_in(stream_key, 6), axis_at), (shards_of,), jnp.float32, low / len(pieces), largest / len(pieces))
        gain = gain * jnp.repeat(jnp.exp(steps), dims[axis_at] // shards_of).reshape((-1,) + (1,) * (len(dims) - 1 - axis_at))
    return gain


def split_up(amount, total, limit, slope):
    weights = [(1 << 20) // math.isqrt(rank ** slope) + 1 for rank in range(2, amount + 1)]
    surplus, holding = total - limit - (amount - 1), [1] * (amount - 1)
    while surplus > 0:
        free = [i for i in range(amount - 1) if holding[i] < limit]
        whole, budget = sum([weights[i] for i in free]), surplus
        for i in free:
            addition = min(limit - holding[i], max(1, budget * weights[i] // whole), surplus)
            holding[i] = holding[i] + addition
            surplus = surplus - addition
    return np.array([limit] + holding)


def uneven_parts(key, number_of, total, bound, skew):
    if number_of == 2:
        one = jax.random.randint(key, (), max(1, total - bound), min(bound, total - 1) + 1)
        return jnp.stack([one, total - one])
    lengths = jnp.asarray(split_up(number_of, total, bound, skew), jnp.int32)
    pairs = (number_of - 1) // 2
    giver, sink = lengths[1:1 + 2 * pairs:2], lengths[2:2 + 2 * pairs:2]
    room = jnp.minimum(giver - 1, bound - sink)
    shifted = jax.random.randint(jax.random.fold_in(key, 1), (pairs,), 0, 1 << 20) % (room + 1)
    lengths = lengths.at[1:1 + 2 * pairs:2].set(giver - shifted).at[2:2 + 2 * pairs:2].set(sink + shifted)
    return lengths[jax.random.permutation(jax.random.fold_in(key, 2), number_of)]


def noise(rng, dims, width, limit, pieces=(), kind=jnp.bfloat16):
    level = block_levels(rng, dims, pieces, -0.22, 0.18) if pieces else 1.0
    values = jax.random.normal(rng, dims, jnp.float32) * width * level
    return jnp.minimum(jnp.maximum(values, -limit), limit).astype(kind)


def setup_inputs(seed: int = 0) -> dict:
    arg_keys = jax.random.split(jax.random.key(seed), 12)
    tokens = noise(arg_keys[0], (TOKENS, D), 1.0, 6.0, ((0, 128),))
    q_weight = draw_q_weight(jax.random.fold_in(arg_keys[11], 71), 0)
    k_weight = draw_k_weight(jax.random.fold_in(arg_keys[11], 71), 0)
    v_weight = noise(arg_keys[3], (D, KVH * HD), D ** -0.5, 0.125, ((1, 4),))
    o_weight = noise(arg_keys[4], (QH * HD, D), (QH * HD) ** -0.5, 0.1875, ((0, 4),))
    kv_pages = draw_kv_pages(jax.random.fold_in(arg_keys[11], 71), 0)
    page_node = draw_page_node(jax.random.fold_in(arg_keys[11], 71), 0)
    page_fill = with_ends(jax.random.randint(arg_keys[7], (PAGES,), 1, PAGE + 1), jax.random.fold_in(arg_keys[7], 1), 1, PAGE).astype(jnp.int32)
    req_len = uneven_parts(arg_keys[8], REQS, TOKENS, PROMPT, 2).astype(jnp.int32)
    req_leaf = with_ends(jax.random.randint(arg_keys[9], (REQS,), 0, LEAVES), jax.random.fold_in(arg_keys[9], 1), 0, LEAVES - 1).astype(jnp.int32)
    leaf_parent = with_ends(jax.random.randint(arg_keys[10], (LEAVES,), 0, MIDS), jax.random.fold_in(arg_keys[10], 1), 0, MIDS - 1).astype(jnp.int32)
    return {"tokens": tokens, "q_weight": q_weight, "k_weight": k_weight, "v_weight": v_weight, "o_weight": o_weight, "kv_pages": kv_pages, "page_node": page_node, "page_fill": page_fill, "req_len": req_len, "req_leaf": req_leaf, "leaf_parent": leaf_parent}


NEGATIVE = -1e+30
EPSILON = 1e-06
ROPE_BASE = 10000.0
SCORE_SCALE = 0.125

def norm_rows(hidden):
    wide = hidden.astype(jnp.float32)
    return (wide * lax.rsqrt(lax.optimization_barrier(jnp.mean(wide * wide, axis=-1, keepdims=True)) + EPSILON)).astype(jnp.bfloat16)

def rotate(values, positions):
    half_dim = values.shape[-1] // 2
    frequency = ROPE_BASE ** (-jnp.arange(half_dim).astype(jnp.float32) / half_dim)
    angles = positions.astype(jnp.float32)[:, None] * frequency[None, :]
    cosine = jnp.cos(angles)[:, None, :]
    sine_part = jnp.sin(angles)[:, None, :]
    first_half = values[..., :half_dim]
    second = values[..., half_dim:]
    return jnp.concatenate([first_half * cosine - second * sine_part, second * cosine + first_half * sine_part], axis=-1)

def request_of(places, req_len):
    req_end = jnp.cumsum(req_len).astype(jnp.int32)
    return lax.optimization_barrier(jnp.sum((places[:, None] >= req_end[None, :]).astype(jnp.int32), axis=1)).astype(jnp.int32)

def row_paths(places, req_len, req_leaf, leaf_parent, page_node, page_fill):
    req_count = req_len.shape[0]
    leaf_count = leaf_parent.shape[0]
    node_count = 1 + MIDS + leaf_count
    starts = (jnp.cumsum(req_len) - req_len).astype(jnp.int32)
    request = request_of(places, req_len)
    chosen = request[:, None] == jnp.arange(req_count, dtype=jnp.int32)[None, :]
    offset = places - lax.optimization_barrier(jnp.sum(jnp.where(chosen, starts[None, :], 0), axis=1)).astype(jnp.int32)
    leaf_id = lax.optimization_barrier(jnp.sum(jnp.where(chosen, req_leaf[None, :], 0), axis=1)).astype(jnp.int32)
    leaf_hit = leaf_id[:, None] == jnp.arange(leaf_count, dtype=jnp.int32)[None, :]
    mid_id = lax.optimization_barrier(jnp.sum(jnp.where(leaf_hit, leaf_parent[None, :], 0), axis=1)).astype(jnp.int32)
    path_ids = jnp.stack([jnp.zeros_like(mid_id), 1 + mid_id, 1 + MIDS + leaf_id], axis=1)
    node_hit = page_node[:, None] == jnp.arange(node_count, dtype=jnp.int32)[None, :]
    node_len = lax.optimization_barrier(jnp.sum(jnp.where(node_hit, page_fill[:, None], 0), axis=0)).astype(jnp.int32)
    on_path = path_ids[:, :, None] == jnp.arange(node_count, dtype=jnp.int32)[None, None, :]
    prefix = lax.optimization_barrier(jnp.sum(jnp.where(on_path, node_len[None, None, :], 0), axis=(1, 2))).astype(jnp.int32)
    return (request, path_ids, prefix + offset)

def page_mask(path_ids, nodes_here, fills_here, page_len):
    node_hit = jnp.any(path_ids[:, :, None] == nodes_here[None, None, :], axis=1)
    slot_live = jnp.arange(page_len, dtype=jnp.int32)[None, :] < fills_here[:, None]
    return (node_hit[:, :, None] & slot_live[None, :, :]).reshape(path_ids.shape[0], -1)

def reference(tokens, q_weight, k_weight, v_weight, o_weight, kv_pages, page_node, page_fill, req_len, req_leaf, leaf_parent):
    group_size = QH // KVH
    highest = lax.Precision.HIGHEST
    normed = norm_rows(tokens)
    places = jnp.arange(TOKENS, dtype=jnp.int32)
    request, path_ids, positions = row_paths(places, req_len, req_leaf, leaf_parent, page_node, page_fill)
    queries = jnp.dot(normed, q_weight, preferred_element_type=jnp.float32).reshape(TOKENS, QH, HD)
    queries = lax.optimization_barrier(rotate(queries, positions).astype(jnp.bfloat16))
    queries = queries.astype(jnp.float32).reshape(TOKENS, KVH, group_size, HD)
    keys_new = jnp.dot(normed, k_weight, preferred_element_type=jnp.float32).reshape(TOKENS, KVH, HD)
    keys_new = lax.optimization_barrier(rotate(keys_new, positions).astype(jnp.bfloat16))
    values_new = jnp.dot(normed, v_weight, preferred_element_type=jnp.float32).reshape(TOKENS, KVH, HD)
    values_new = lax.optimization_barrier(values_new.astype(jnp.bfloat16))
    pad_rows = jnp.zeros((PROMPT, KVH, HD), jnp.bfloat16)
    pad_keys = jnp.concatenate([pad_rows, keys_new], axis=0).astype(jnp.float32)
    pad_values = jnp.concatenate([pad_rows, values_new], axis=0).astype(jnp.float32)
    cache_all = kv_pages.reshape(KVH, PAGES * PAGE, 2 * HD).astype(jnp.float32)
    cache_keys = cache_all[..., :HD]
    cache_values = cache_all[..., HD:]
    row_block = math.gcd(TOKENS, 32)

    def one_block(block_index):
        first_row = block_index * row_block
        q_block = lax.dynamic_slice_in_dim(queries, first_row, row_block, 0)
        req_block = lax.dynamic_slice_in_dim(request, first_row, row_block, 0)
        path_block = lax.dynamic_slice_in_dim(path_ids, first_row, row_block, 0)
        rows_at = first_row + jnp.arange(row_block, dtype=jnp.int32)
        cache_ok = page_mask(path_block, page_node, page_fill, PAGE)
        near_keys = lax.dynamic_slice_in_dim(pad_keys, first_row, PROMPT + row_block, 0)
        near_values = lax.dynamic_slice_in_dim(pad_values, first_row, PROMPT + row_block, 0)
        near_place = first_row - PROMPT + jnp.arange(PROMPT + row_block, dtype=jnp.int32)
        near_req = request_of(jnp.maximum(near_place, 0), req_len)
        near_ok = (near_place[None, :] >= 0) & (near_req[None, :] == req_block[:, None]) & (near_place[None, :] <= rows_at[:, None])
        s_cache = jnp.einsum('rkhd,knd->khrn', q_block, cache_keys, precision=highest) * SCORE_SCALE
        s_near = jnp.einsum('rkhd,nkd->khrn', q_block, near_keys, precision=highest) * SCORE_SCALE
        s_cache = jnp.where(cache_ok[None, None], s_cache, NEGATIVE)
        s_near = jnp.where(near_ok[None, None], s_near, NEGATIVE)
        row_top = jnp.maximum(lax.optimization_barrier(jnp.max(s_cache, axis=-1)), lax.optimization_barrier(jnp.max(s_near, axis=-1)))
        p_cache = jnp.where(cache_ok[None, None], jnp.exp(s_cache - row_top[..., None]), 0.0)
        p_near = jnp.where(near_ok[None, None], jnp.exp(s_near - row_top[..., None]), 0.0)
        row_total = lax.optimization_barrier(jnp.sum(p_cache, axis=-1)) + lax.optimization_barrier(jnp.sum(p_near, axis=-1))
        w_cache = lax.optimization_barrier(p_cache.astype(jnp.bfloat16)).astype(jnp.float32)
        w_near = lax.optimization_barrier(p_near.astype(jnp.bfloat16)).astype(jnp.float32)
        numerator = jnp.einsum('khrn,knd->khrd', w_cache, cache_values, precision=highest)
        numerator = numerator + jnp.einsum('khrn,nkd->khrd', w_near, near_values, precision=highest)
        attended = numerator / row_total[..., None]
        return jnp.transpose(attended, (2, 0, 1, 3)).reshape(row_block, QH * HD).astype(jnp.bfloat16)
    blocks = lax.map(one_block, jnp.arange(TOKENS // row_block, dtype=jnp.int32))
    attended_all = blocks.reshape(TOKENS, QH * HD)
    return jnp.dot(attended_all, o_weight, preferred_element_type=jnp.float32).astype(jnp.bfloat16)
```

```python
import functools

import jax
import jax.numpy as jnp
import numpy as np
from jax import lax
from jax.experimental import pallas as pl
from jax.experimental.pallas import tpu as pltpu
from jax.sharding import PartitionSpec as P

HD = 64
MIDS = 8
LANES = 128
LINES = {128: (8, 8), 8: (2, 2)}
NEGATIVE = -1e30
EPSILON = 1e-06
ROPE_BASE = 10000.0
SCORE_SCALE = 0.125
MESH = pl.DeviceIdType.MESH
F32 = jnp.float32
BF16 = jnp.bfloat16
I32 = jnp.int32


def offset_at(place, count):
    if isinstance(place, int):
        half = (place + 1) // 2
        return half if place % 2 else (count - half) % count
    half = lax.div(place + 1, 2)
    odd = lax.rem(place, 2)
    return lax.rem(odd * half + (1 - odd) * (count - half), count)


def mirror(place, count):
    if isinstance(place, int):
        if place in (0, count - 1):
            return place
        return place + 1 if place % 2 else place - 1
    odd = lax.rem(place, 2)
    ends = jnp.logical_or(place == 0, place == count - 1)
    return jnp.where(ends, place, place + 2 * odd - 1)


def iota(shape, axis):
    return lax.broadcasted_iota(I32, shape, axis)


def kernel(
    sizes,
    tok,
    wq,
    wk,
    wv,
    wo,
    pages,
    node_hbm,
    fill_hbm,
    len_hbm,
    leaf_hbm,
    parent_hbm,
    freq_hbm,
    out,
    tok_v,
    wq_v,
    wk_v,
    wv_v,
    node_s,
    fill_s,
    node_v,
    fill_v,
    len_v,
    leaf_v,
    parent_v,
    freq_v,
    kvb,
    keys,
    vals,
    near,
    qbuf,
    hot,
    qaug,
    state_top,
    state_sum,
    part,
    part_lse,
    got,
    got_lse,
    own_part,
    att,
    wob,
    loc,
    kv_ss,
    kv_rs,
    fw_ss,
    fw_rs,
    q_ss,
    q_rs,
    nr_ss,
    nr_rs,
    o_ss,
    o_rs,
    l_ss,
    l_rs,
    w_ss,
    w_rs,
    a_ss,
    a_rs,
):
    nx, ny, nz, rows, heads = sizes
    group = heads * rows
    out_cols = out.shape[1]
    n_blk = ny * nz * 2
    hx = lax.axis_index("head")
    blk = lax.axis_index("blk")
    core = lax.rem(blk, 2)
    zi = lax.rem(lax.div(blk, 2), nz)
    yi = lax.div(blk, 2 * nz)

    def blk_of(y, z, c):
        return (y * nz + z) * 2 + c

    def y_peer(place):
        return blk_of(lax.rem(yi + offset_at(place, ny), ny), zi, core)

    def z_peer(place):
        return blk_of(yi, lax.rem(zi + offset_at(place, nz), nz), core)

    sibling = blk_of(yi, zi, 1 - core)

    barrier = pltpu.get_barrier_semaphore()
    greeted = [sibling]
    greeted += [y_peer(place) for place in range(1, ny)]
    greeted += [z_peer(place) for place in range(1, nz)]
    for step in range(1, 5):
        if step < n_blk:
            greeted += [lax.rem(blk + step, n_blk), lax.rem(blk + n_blk - step, n_blk)]
    for peer in greeted:
        pl.semaphore_signal(barrier, inc=1, device_id=(hx, peer), device_id_type=MESH)
    for step in range(1, nx):
        pl.semaphore_signal(
            barrier, inc=1, device_id=(lax.rem(hx + step, nx), blk), device_id_type=MESH
        )

    copies = [
        pltpu.make_async_copy(src, dst, loc.at[at])
        for at, (src, dst) in enumerate(
            [
                (len_hbm, len_v),
                (leaf_hbm, leaf_v),
                (parent_hbm, parent_v),
                (node_hbm, node_v),
                (fill_hbm, fill_v),
                (freq_hbm, freq_v),
                (node_hbm.at[0], node_s),
                (fill_hbm.at[0], fill_s),
                (tok, tok_v),
                (wq, wq_v),
                (wk, wk_v),
                (wv, wv_v),
                (pages.at[0], kvb.at[0]),
                (wo.at[:, pl.ds(pl.multiple_of(hx * out_cols, LANES), out_cols)], wob.at[hx]),
            ]
        )
    ]
    for copy in copies:
        copy.start()

    def remote(src, dst, send, recv, to_head, to_blk):
        return pltpu.make_async_remote_copy(
            src_ref=src,
            dst_ref=dst,
            send_sem=send,
            recv_sem=recv,
            device_id=(to_head, to_blk),
            device_id_type=MESH,
        )

    def kv_copy(place):
        back = mirror(place, ny)
        return remote(
            pages.at[0], kvb.at[2 * back], kv_ss.at[place], kv_rs.at[back], hx, y_peer(place)
        )

    def forward(place):
        src = pages.at[0] if isinstance(place, int) and place == 0 else kvb.at[2 * place]
        return remote(src, kvb.at[2 * place + 1], fw_ss.at[place], fw_rs.at[place], hx, sibling)

    def wo_copy(step):
        to = lax.rem(hx + step, nx)
        cols = pl.ds(pl.multiple_of(to * out_cols, LANES), out_cols)
        return remote(wo.at[:, cols], wob.at[hx], w_ss.at[step], w_rs.at[step], to, blk)

    def near_copy(step):
        to = lax.rem(blk + step, n_blk)
        return remote(near.at[4], near.at[4 - step], nr_ss.at[step], nr_rs.at[step], hx, to)

    def q_copy(place):
        back = mirror(place, nz)
        return remote(
            qbuf.at[0], qbuf.at[back], q_ss.at[place], q_rs.at[back], hx, z_peer(place)
        )

    def part_copies(place):
        back = mirror(place, nz)
        to = z_peer(place)
        return (
            remote(part.at[place], got.at[back], o_ss.at[place], o_rs.at[back], hx, to),
            remote(part_lse.at[place], got_lse.at[back], l_ss.at[place], l_rs.at[back], hx, to),
        )

    def att_copy(step):
        to = lax.rem(hx + step, nx)
        return remote(att.at[hx], att.at[hx], a_ss.at[step], a_rs.at[step], to, blk)

    pl.semaphore_wait(barrier, len(greeted) + nx - 1)
    for place in range(1, ny):
        kv_copy(place).start()
    forward(0).start()
    for step in range(1, nx):
        wo_copy(step).start()

    for copy in copies[:6]:
        copy.wait()
    reqs = len_v.shape[1]
    leaves = parent_v.shape[1]
    diag = iota((reqs, reqs), 0) == iota((reqs, reqs), 1)

    def to_column(row):
        return jnp.sum(jnp.where(diag, row, 0), axis=1, keepdims=True)

    def to_row(column):
        return jnp.sum(jnp.where(diag, column, 0), axis=0, keepdims=True)

    len_row = len_v[...]
    len_col = to_column(len_row)
    upto = iota((reqs, reqs), 0) <= iota((reqs, reqs), 1)
    end_row = jnp.sum(jnp.where(upto, len_col, 0), axis=0, keepdims=True)
    start_row = end_row - len_row
    leaf_col = to_column(leaf_v[...])
    leaf_hit = leaf_col == iota((reqs, leaves), 1)
    mid_col = jnp.sum(jnp.where(leaf_hit, parent_v[...], 0), axis=1, keepdims=True)
    node_row = node_v[...]
    on_path = (node_row == 0) | (node_row == 1 + mid_col) | (node_row == 1 + MIDS + leaf_col)
    prefix_col = jnp.sum(jnp.where(on_path, fill_v[...], 0), axis=1, keepdims=True)
    shift_row = to_row(prefix_col) - start_row
    lane_req = iota((reqs, LANES), 1) - HD
    path_hot = (
        (lane_req == mid_col)
        & (lane_req < MIDS)
        | (lane_req - MIDS == lax.shift_right_logical(leaf_col, 3)) & (lane_req < 2 * MIDS)
        | (lane_req - 2 * MIDS == (leaf_col & 7)) & (lane_req < 3 * MIDS)
    ) & (lane_req >= 0)
    path_table = jnp.where(path_hot, 1.0, 0.0).astype(BF16)

    def requests_of(device):
        place = device * rows + iota((rows, reqs), 0)
        return (place >= start_row) & (place < end_row)

    own_hit = requests_of(blk)
    own_place = blk * rows + iota((rows, 1), 0)
    own_start = jnp.sum(jnp.where(own_hit, start_row, 0), axis=1, keepdims=True)
    position = own_place + jnp.sum(jnp.where(own_hit, shift_row, 0), axis=1, keepdims=True)
    angles = position.astype(F32) * freq_v[...]
    cosine = jnp.cos(angles)
    sine = jnp.sin(angles)
    lane = iota((rows, LANES), 1)
    first_half = lax.rem(lane, HD) < HD // 2
    sine = jnp.where(first_half, -sine, sine)
    low = lane < HD

    def rotated(v, cos, sin):
        swapped = jnp.where(
            first_half,
            pltpu.roll(v, LANES - HD // 2, 1),
            pltpu.roll(v, HD // 2, 1),
        )
        return v * cos + swapped * sin

    copies[8].wait()
    wide = tok_v[...].astype(F32)
    normed = (wide * lax.rsqrt(jnp.mean(wide * wide, axis=1, keepdims=True) + EPSILON)).astype(BF16)
    copies[9].wait()
    queries = jnp.dot(normed, wq_v[...], preferred_element_type=F32)
    for half in range(heads // 2):
        turned = rotated(queries[:, half * LANES : (half + 1) * LANES], cosine, sine)
        qbuf[0, :, half * LANES : (half + 1) * LANES] = turned.astype(BF16) * SCORE_SCALE
    for place in range(1, nz):
        q_copy(place).start()
    copies[10].wait()
    copies[11].wait()
    keys_new = jnp.dot(normed, wk_v[...], preferred_element_type=F32)
    values_new = jnp.dot(normed, wv_v[...], preferred_element_type=F32)
    pack = jnp.concatenate([keys_new, values_new], axis=1)
    pack = rotated(pack, jnp.where(low, cosine, 1.0), jnp.where(low, sine, 0.0))
    near[4] = pack.astype(BF16)
    for step in range(1, 5):
        near_copy(step).start()

    @pl.loop(0, nz)
    def _(place):
        hit = jnp.where(requests_of(z_peer(place)), 1.0, 0.0).astype(BF16)
        hot[place] = jnp.dot(hit, path_table, preferred_element_type=F32).astype(BF16)

    copies[6].wait()
    copies[7].wait()
    page_len = pages.shape[2]
    per_slot = pages.shape[1]
    lane_page = iota((page_len, LANES), 1) - HD
    slot_at = iota((page_len, LANES), 0)

    @pl.loop(0, 2 * ny)
    def _(slot):
        place = lax.div(slot, 2)
        other = lax.rem(slot, 2)
        source = blk_of(
            lax.rem(yi + offset_at(place, ny), ny), zi, core + other - 2 * core * other
        )
        for page in range(per_slot):
            node = node_s[source * per_slot + page]
            used = fill_s[source * per_slot + page]
            node = jnp.full((page_len, LANES), node, I32)
            leaf = node - 1 - MIDS
            is_mid = (node >= 1) & (leaf < 0)
            is_leaf = leaf >= 0
            bad = (
                (lane_page >= 0)
                & (lane_page < MIDS)
                & ((slot_at >= used) | (is_mid & (lane_page != node - 1)))
            )
            bad = bad | (
                is_leaf
                & (lane_page >= MIDS)
                & (lane_page < 2 * MIDS)
                & (lane_page - MIDS != lax.shift_right_arithmetic(leaf, 3))
            )
            bad = bad | (
                is_leaf
                & (lane_page >= 2 * MIDS)
                & (lane_page < 3 * MIDS)
                & (lane_page - 2 * MIDS != (leaf & 7))
            )
            at = pl.multiple_of((slot * per_slot + page) * page_len, page_len)
            keys[pl.ds(at, page_len), :] = jnp.where(bad, NEGATIVE, 0.0).astype(BF16)

    vals[HD:, :] = jnp.ones((vals.shape[0] - HD, vals.shape[1]), BF16)
    low_one = jnp.where(low[:1], 1.0, 0.0).astype(BF16)

    def build_queries(place):
        for half in range(heads // 2):
            two = qbuf[place, :, half * LANES : (half + 1) * LANES]
            turned = pltpu.roll(two.astype(F32), HD, 1).astype(BF16)
            extra = hot[place]
            base = 2 * half * rows
            qaug[place, base : base + rows, :] = two * low_one + extra
            qaug[place, base + rows : base + 2 * rows, :] = turned * low_one + extra

    slot_keys = per_slot * page_len

    def build_keys(place):
        span = slice(2 * place * slot_keys, 2 * (place + 1) * slot_keys)
        both = kvb[2 * place : 2 * place + 2].reshape(2 * slot_keys, LANES)
        keys[span, :] = both * low_one + keys[span, :]
        vals[0:HD, span] = both.astype(F32).T[HD:].astype(BF16)

    def attend(query, key, value):
        scores = lax.dot_general(key, query, (((1,), (1,)), ((), ())), preferred_element_type=F32)
        return scores, value

    def fold(scores, value):
        top = jnp.max(scores, axis=0, keepdims=True)
        weights = jnp.exp(scores - top).astype(BF16)
        return top, jnp.dot(value, weights, preferred_element_type=F32)

    half_places = ny // 2
    for place in range(1, half_places):
        kv_copy(mirror(place, ny)).wait_recv()
        forward(place).start()

    build_queries(0)

    for step in range(1, 5):
        near_copy(step).wait_recv()
    near_rows = 5 * rows
    near_all = near[...].reshape(near_rows, LANES)
    near_scores = lax.dot_general(
        near_all * low_one, qaug[0], (((1,), (1,)), ((), ())), preferred_element_type=F32
    )
    start_lane = jnp.sum(
        jnp.where(
            iota((rows, group), 0) == lax.rem(iota((rows, group), 1), rows), own_start, 0
        ),
        axis=0,
        keepdims=True,
    )
    key_place = (blk - 4) * rows + iota((near_rows, group), 0)
    row_place = blk * rows + lax.rem(iota((near_rows, group), 1), rows)
    allowed = (key_place >= start_lane) & (key_place <= row_place)
    near_scores = jnp.where(allowed, near_scores, NEGATIVE)
    near_values = jnp.concatenate(
        [near_all.astype(F32).T[HD:].astype(BF16), jnp.ones((16, near_rows), BF16)], axis=0
    )
    near_top, near_sum = fold(near_scores, near_values)
    near_total = near_sum[HD : HD + 1]
    near_out = near_sum[0:HD] / near_total
    near_lse = near_top + jnp.log(near_total)

    copies[12].wait()
    for place in range(half_places):
        forward(place).wait_recv()
        build_keys(place)
    first_keys = 2 * half_places * slot_keys
    all_keys = 2 * ny * slot_keys

    @pl.loop(0, nz)
    def _(place):
        @pl.when(place > 0)
        def _():
            q_copy(mirror(place, nz)).wait_recv()
            build_queries(place)

        scores, value = attend(qaug[place], keys[0:first_keys, :], vals[:, 0:first_keys])
        top, total = fold(scores, value)
        state_top[place] = jnp.broadcast_to(top, (8, group))
        state_sum[place] = total

        @pl.when(place >= nz - (ny - half_places))
        def _():
            line = place - nz + ny
            kv_copy(mirror(line, ny)).wait_recv()
            forward(line).start()

    for place in range(half_places, ny):
        forward(place).wait_recv()
        build_keys(place)

    @pl.loop(0, nz)
    def _(turn):
        place = nz - 1 - turn
        scores, value = attend(
            qaug[place], keys[first_keys:all_keys, :], vals[:, first_keys:all_keys]
        )
        top, total = fold(scores, value)
        old_top = state_top[place][0:1]
        new_top = jnp.maximum(top, old_top)
        total = total * jnp.exp(top - new_top) + state_sum[place] * jnp.exp(old_top - new_top)
        mass = total[HD : HD + 1]
        result = total[0:HD] / mass
        lse = jnp.broadcast_to(new_top + jnp.log(mass), (8, group))
        part[place] = result.astype(BF16)
        part_lse[place] = lse
        own_part[...] = result

        @pl.when(place > 0)
        def _():
            for copy in part_copies(place):
                copy.start()

    lses = [near_lse, part_lse[0][0:1]]
    for place in range(1, nz):
        for copy in part_copies(mirror(place, nz)):
            copy.wait_recv()
        lses.append(got_lse[place][0:1])
    top = functools.reduce(jnp.maximum, lses)
    shares = [jnp.exp(lse - top) for lse in lses]
    scale = 1.0 / functools.reduce(jnp.add, shares)
    joined = near_out * (shares[0] * scale) + own_part[...] * (shares[1] * scale)
    for place in range(1, nz):
        joined = joined + got[place].astype(F32) * (shares[place + 1] * scale)
    for half in range(heads // 2):
        two = joined[:, half * LANES : (half + 1) * LANES]
        square = jnp.concatenate([two, pltpu.roll(two, rows, 1)], axis=0)
        att[hx, :, half * LANES : (half + 1) * LANES] = square.T[0:rows].astype(BF16)
    for step in range(1, nx):
        att_copy(step).start()

    copies[13].wait()
    total = jnp.dot(att[hx], wob[hx], preferred_element_type=F32)
    for step in range(1, nx):
        wo_copy(step).wait_recv()
        att_copy(step).wait_recv()
        source = lax.rem(hx + nx - step, nx)
        total = total + jnp.dot(att[source], wob[source], preferred_element_type=F32)
    out[...] = total.astype(BF16)

    for place in range(1, ny):
        kv_copy(place).wait_send()
    for place in range(ny):
        forward(place).wait_send()
    for place in range(1, nz):
        q_copy(place).wait_send()
        for copy in part_copies(place):
            copy.wait_send()
    for step in range(1, 5):
        near_copy(step).wait_send()
    for step in range(1, nx):
        wo_copy(step).wait_send()
        att_copy(step).wait_send()


def local(
    tokens, q_weight, k_weight, v_weight, o_weight, kv_pages, page_node, page_fill, req_len, req_leaf, leaf_parent
):
    nx = lax.axis_size("head")
    ny, nz = LINES[lax.axis_size("blk")]
    rows, width = tokens.shape
    heads = q_weight.shape[1] // HD
    group = heads * rows
    out_cols = o_weight.shape[1] // nx
    per_slot, page_len = kv_pages.shape[1:3]
    slots = 2 * ny
    all_keys = slots * per_slot * page_len
    pages = page_node.shape[0]
    reqs = req_len.shape[0]
    leaves = leaf_parent.shape[0]
    half = HD // 2
    freq = np.tile(ROPE_BASE ** (-np.arange(half) / half), LANES // half)[None, :]
    dma = pltpu.SemaphoreType.DMA
    scratch = [
        pltpu.VMEM((rows, width), BF16),
        pltpu.VMEM((width, heads * HD), BF16),
        pltpu.VMEM((width, HD), BF16),
        pltpu.VMEM((width, HD), BF16),
        pltpu.SMEM((pages,), I32),
        pltpu.SMEM((pages,), I32),
        pltpu.VMEM((1, pages), I32),
        pltpu.VMEM((1, pages), I32),
        pltpu.VMEM((1, reqs), I32),
        pltpu.VMEM((1, reqs), I32),
        pltpu.VMEM((1, leaves), I32),
        pltpu.VMEM((1, LANES), F32),
        pltpu.VMEM((slots, per_slot, page_len, LANES), BF16),
        pltpu.VMEM((all_keys, LANES), BF16),
        pltpu.VMEM((HD + 16, all_keys), BF16),
        pltpu.VMEM((5, rows, LANES), BF16),
        pltpu.VMEM((nz, rows, heads * HD), BF16),
        pltpu.VMEM((nz, rows, LANES), BF16),
        pltpu.VMEM((nz, group, LANES), BF16),
        pltpu.VMEM((nz, 8, group), F32),
        pltpu.VMEM((nz, HD + 16, group), F32),
        pltpu.VMEM((nz, HD, group), BF16),
        pltpu.VMEM((nz, 8, group), F32),
        pltpu.VMEM((nz, HD, group), BF16),
        pltpu.VMEM((nz, 8, group), F32),
        pltpu.VMEM((HD, group), F32),
        pltpu.VMEM((nx, rows, heads * HD), BF16),
        pltpu.VMEM((nx, heads * HD, out_cols), BF16),
        dma((14,)),
        dma((ny,)),
        dma((ny,)),
        dma((ny,)),
        dma((ny,)),
        dma((nz,)),
        dma((nz,)),
        dma((5,)),
        dma((5,)),
        dma((nz,)),
        dma((nz,)),
        dma((nz,)),
        dma((nz,)),
        dma((nx,)),
        dma((nx,)),
        dma((nx,)),
        dma((nx,)),
    ]
    anywhere = pl.BlockSpec(memory_space=pl.ANY)
    return pl.pallas_call(
        functools.partial(kernel, (nx, ny, nz, rows, heads)),
        out_shape=jax.ShapeDtypeStruct((rows, out_cols), BF16),
        in_specs=[anywhere] * 12,
        out_specs=pl.BlockSpec(memory_space=pltpu.VMEM),
        scratch_shapes=scratch,
        compiler_params=pltpu.CompilerParams(
            collective_id=0, has_side_effects=True, vmem_limit_bytes=56 << 20
        ),
        name="tree_attention",
    )(
        tokens,
        q_weight,
        k_weight,
        v_weight,
        o_weight,
        kv_pages,
        page_node[None, :],
        page_fill[None, :],
        req_len[None, :],
        req_leaf[None, :],
        leaf_parent[None, :],
        jnp.asarray(freq, F32),
    )


def solution(mesh):
    return jax.shard_map(
        local,
        mesh=mesh,
        in_specs=(
            P("blk", None),
            P(None, "head"),
            P(None, "head"),
            P(None, "head"),
            P("head", None),
            P("head", "blk", None, None),
            P(),
            P(),
            P(),
            P(),
            P(),
        ),
        out_specs=P("blk", "head"),
        check_vma=False,
    )
```

```python
import functools

import jax
import jax.numpy as jnp
import numpy as np
from jax import lax
from jax.experimental import pallas as pl
from jax.experimental.pallas import tpu as pltpu
from jax.sharding import PartitionSpec as P

HD = 64
MIDS = 8
LANES = 128
LINES = {128: (8, 8), 8: (2, 2)}
NEGATIVE = -1e30
LOWEST = -3e38
EPSILON = 1e-06
ROPE_BASE = 10000.0
SCORE_SCALE = 0.125
MESH = pl.DeviceIdType.MESH
F32 = jnp.float32
BF16 = jnp.bfloat16
I32 = jnp.int32


def offset_at(place, count):
    if isinstance(place, int):
        half = (place + 1) // 2
        return half if place % 2 else (count - half) % count
    half = lax.div(place + 1, 2)
    odd = lax.rem(place, 2)
    return lax.rem(odd * half + (1 - odd) * (count - half), count)


def mirror(place, count):
    if isinstance(place, int):
        if place in (0, count - 1):
            return place
        return place + 1 if place % 2 else place - 1
    odd = lax.rem(place, 2)
    ends = jnp.logical_or(place == 0, place == count - 1)
    return jnp.where(ends, place, place + 2 * odd - 1)


KV_RING, Q_RING, O_RING = False, False, False


def iota(shape, axis):
    return lax.broadcasted_iota(I32, shape, axis)


def kernel(
    sizes,
    tok,
    wq,
    wk,
    wv,
    wo,
    pages,
    node_hbm,
    fill_hbm,
    len_hbm,
    leaf_hbm,
    parent_hbm,
    freq_hbm,
    out,
    tok_v,
    wq_v,
    wkv_v,
    node_s,
    fill_s,
    node_v,
    fill_v,
    len_v,
    leaf_v,
    parent_v,
    freq_v,
    kvb,
    keys,
    vals,
    near,
    qbuf,
    hot,
    qaug,
    state_top,
    state_sum,
    part,
    part_lse,
    got,
    got_lse,
    scores_a,
    scores_b,
    att,
    wob,
    loc,
    kv_ss,
    kv_rs,
    fw_ss,
    fw_rs,
    q_ss,
    q_rs,
    nr_ss,
    nr_rs,
    o_ss,
    o_rs,
    l_ss,
    l_rs,
    w_ss,
    w_rs,
    a_ss,
    a_rs,
):
    nx, ny, nz, rows, heads = sizes
    group = heads * rows
    out_cols = out.shape[1]
    n_blk = ny * nz * 2
    hx = lax.axis_index("head")
    blk = lax.axis_index("blk")
    core = lax.rem(blk, 2)
    zi = lax.rem(lax.div(blk, 2), nz)
    yi = lax.div(blk, 2 * nz)

    def blk_of(y, z, c):
        return (y * nz + z) * 2 + c

    def y_next(step):
        return blk_of(lax.rem(yi + ny + step, ny), zi, core)

    def z_next(step):
        return blk_of(yi, lax.rem(zi + nz + step, nz), core)

    def y_peer(place):
        return blk_of(lax.rem(yi + offset_at(place, ny), ny), zi, core)

    def z_peer(place):
        return blk_of(yi, lax.rem(zi + offset_at(place, nz), nz), core)

    sibling = blk_of(yi, zi, 1 - core)

    copies = [
        pltpu.make_async_copy(src, dst, loc.at[at])
        for at, (src, dst) in enumerate(
            [
                (len_hbm, len_v.at[0]),
                (leaf_hbm, leaf_v.at[0]),
                (parent_hbm, parent_v.at[0]),
                (node_hbm, node_v.at[0]),
                (fill_hbm, fill_v.at[0]),
                (freq_hbm, freq_v),
                (node_hbm, node_s),
                (fill_hbm, fill_s),
                (tok, tok_v),
                (wq, wq_v),
                (wk, wkv_v.at[0:HD]),
                (wv, wkv_v.at[HD:]),
                (pages.at[0], kvb.at[0]),
                (wo.at[:, pl.ds(pl.multiple_of(hx * out_cols, LANES), out_cols)], wob.at[hx]),
            ]
        )
    ]
    for at in (8, 9, 10, 11, 0, 1, 2, 3, 4, 5, 6, 7, 12):
        copies[at].start()

    barrier = pltpu.get_barrier_semaphore()
    greeted = [sibling]
    if KV_RING:
        greeted += [y_next(1), y_next(-1)]
    else:
        greeted += [y_peer(place) for place in range(1, ny)]
    if Q_RING and O_RING:
        greeted += [z_next(1), z_next(-1)]
    else:
        greeted += [z_peer(place) for place in range(1, nz)]
    for step in range(1, 5):
        if step < n_blk:
            greeted += [lax.rem(blk + step, n_blk), lax.rem(blk + n_blk - step, n_blk)]
    for peer in greeted:
        pl.semaphore_signal(barrier, inc=1, device_id=(hx, peer), device_id_type=MESH)
    for step in range(1, nx):
        pl.semaphore_signal(
            barrier, inc=1, device_id=(lax.rem(hx + step, nx), blk), device_id_type=MESH
        )

    def remote(src, dst, send, recv, to_head, to_blk):
        return pltpu.make_async_remote_copy(
            src_ref=src,
            dst_ref=dst,
            send_sem=send,
            recv_sem=recv,
            device_id=(to_head, to_blk),
            device_id_type=MESH,
        )

    def kv_copy(place):
        if not KV_RING:
            back = mirror(place, ny)
            return remote(
                pages.at[0], kvb.at[2 * back], kv_ss.at[place], kv_rs.at[back], hx, y_peer(place)
            )
        src = pages.at[0] if place <= 2 else kvb.at[2 * (place - 2)]
        to = y_next(-1 if place % 2 else 1)
        return remote(src, kvb.at[2 * place], kv_ss.at[place], kv_rs.at[place], hx, to)

    def forward(place):
        src = kvb.at[2 * place] if place else pages.at[0]
        return remote(src, kvb.at[2 * place + 1], fw_ss.at[place], fw_rs.at[place], hx, sibling)

    def pass_pages(hops):
        for place in (2 * hops - 1, 2 * hops):
            if place < ny:
                kv_copy(place if KV_RING else mirror(place, ny)).wait_recv()
                if KV_RING and place + 2 < ny:
                    kv_copy(place + 2).start()
                forward(place).start()

    def wo_copy(step):
        to = lax.rem(hx + step, nx)
        cols = pl.ds(pl.multiple_of(to * out_cols, LANES), out_cols)
        return remote(wo.at[:, cols], wob.at[hx], w_ss.at[step], w_rs.at[step], to, blk)

    def near_copy(step):
        to = lax.rem(blk + step, n_blk)
        return remote(near.at[4], near.at[4 - step], nr_ss.at[step], nr_rs.at[step], hx, to)

    def q_copy(place):
        if not Q_RING:
            back = mirror(place, nz)
            return remote(
                qbuf.at[0], qbuf.at[back], q_ss.at[place], q_rs.at[back], hx, z_peer(place)
            )
        odd = lax.rem(place, 2)
        src = qbuf.at[jnp.maximum(place - 2, 0)]
        to = z_next(1 - 2 * odd)
        return remote(src, qbuf.at[place], q_ss.at[place], q_rs.at[place], hx, to)

    def part_copies(place):
        if not O_RING:
            back = mirror(place, nz)
            to = z_peer(place)
            return (
                remote(part.at[place], got.at[back], o_ss.at[place], o_rs.at[back], hx, to),
                remote(part_lse.at[place], got_lse.at[back], l_ss.at[place], l_rs.at[back], hx, to),
            )
        to = z_next(2 * lax.rem(place, 2) - 1)
        return (
            remote(part.at[place], got.at[place], o_ss.at[place], o_rs.at[place], hx, to),
            remote(part_lse.at[place], got_lse.at[place], l_ss.at[place], l_rs.at[place], hx, to),
        )

    def att_copy(step):
        to = lax.rem(hx + step, nx)
        return remote(att.at[hx], att.at[hx], a_ss.at[step], a_rs.at[step], to, blk)

    pl.semaphore_wait(barrier, len(greeted) + nx - 1)
    for place in (1, 2) if KV_RING else range(1, ny):
        if place < ny:
            kv_copy(place).start()
    forward(0).start()

    for copy in copies[:6]:
        copy.wait()
    reqs = len_v.shape[1]
    leaves = parent_v.shape[1]
    diag = iota((reqs, reqs), 0) == iota((reqs, reqs), 1)

    def to_column(row):
        return jnp.sum(jnp.where(diag, row, 0), axis=1, keepdims=True)

    def to_row(column):
        return jnp.sum(jnp.where(diag, column, 0), axis=0, keepdims=True)

    len_row = len_v[...]
    len_col = to_column(len_row)
    upto = iota((reqs, reqs), 0) <= iota((reqs, reqs), 1)
    end_row = jnp.sum(jnp.where(upto, len_col, 0), axis=0, keepdims=True)
    start_row = end_row - len_row
    leaf_col = to_column(leaf_v[...])
    leaf_hit = leaf_col == iota((reqs, leaves), 1)
    mid_col = jnp.sum(jnp.where(leaf_hit, parent_v[...], 0), axis=1, keepdims=True)
    node_row = node_v[...]
    on_path = (node_row == 0) | (node_row == 1 + mid_col) | (node_row == 1 + MIDS + leaf_col)
    prefix_col = jnp.sum(jnp.where(on_path, fill_v[...], 0), axis=1, keepdims=True)
    shift_row = to_row(prefix_col) - start_row
    lane_req = iota((reqs, LANES), 1) - HD
    path_hot = (
        (lane_req == mid_col)
        & (lane_req < MIDS)
        | (lane_req - MIDS == lax.shift_right_logical(leaf_col, 3)) & (lane_req < 2 * MIDS)
        | (lane_req - 2 * MIDS == (leaf_col & 7)) & (lane_req < 3 * MIDS)
    ) & (lane_req >= 0)
    path_table = jnp.where(path_hot, 1.0, 0.0).astype(BF16)

    def requests_of(device):
        place = device * rows + iota((rows, reqs), 0)
        return (place >= start_row) & (place < end_row)

    own_hit = requests_of(blk)
    own_place = blk * rows + iota((rows, 1), 0)
    own_start = jnp.sum(jnp.where(own_hit, start_row, 0), axis=1, keepdims=True)
    position = own_place + jnp.sum(jnp.where(own_hit, shift_row, 0), axis=1, keepdims=True)
    angles = position.astype(F32) * freq_v[...]
    cosine = jnp.cos(angles)
    sine = jnp.sin(angles)
    lane = iota((rows, LANES), 1)
    first_half = lax.rem(lane, HD) < HD // 2
    sine = jnp.where(first_half, -sine, sine)
    low = lane < HD

    def rotated(v, cos, sin):
        swapped = jnp.where(
            first_half,
            pltpu.roll(v, LANES - HD // 2, 1),
            pltpu.roll(v, HD // 2, 1),
        )
        return v * cos + swapped * sin

    pass_pages(1)

    copies[8].wait()
    wide = tok_v[...].astype(F32)
    normed = (wide * lax.rsqrt(jnp.mean(wide * wide, axis=1, keepdims=True) + EPSILON)).astype(BF16)
    copies[9].wait()
    queries = jnp.dot(normed, wq_v[...], preferred_element_type=F32)
    for half in range(heads // 2):
        turned = rotated(queries[:, half * LANES : (half + 1) * LANES], cosine, sine)
        qbuf[0, :, half * LANES : (half + 1) * LANES] = turned.astype(BF16) * SCORE_SCALE
    for place in (1, 2) if Q_RING else range(1, nz):
        if place < nz:
            q_copy(place).start()
    copies[10].wait()
    copies[11].wait()
    pack = lax.dot_general(
        normed, wkv_v[...], (((1,), (1,)), ((), ())), preferred_element_type=F32
    )
    pack = rotated(pack, jnp.where(low, cosine, 1.0), jnp.where(low, sine, 0.0))
    near[4] = pack.astype(BF16)
    for step in range(1, 5):
        near_copy(step).start()
    copies[13].start()
    for step in range(1, nx):
        wo_copy(step).start()

    pass_pages(2)

    @pl.loop(0, nz)
    def _(place):
        hit = jnp.where(requests_of(z_next(offset_at(place, nz))), 1.0, 0.0).astype(BF16)
        hot[place] = jnp.dot(hit, path_table, preferred_element_type=F32).astype(BF16)

    copies[6].wait()
    copies[7].wait()
    page_len = pages.shape[2]
    per_slot = pages.shape[1]
    lane_page = iota((page_len, LANES), 1) - HD
    slot_at = iota((page_len, LANES), 0)

    @pl.loop(0, 2 * ny)
    def _(slot):
        place = lax.div(slot, 2)
        other = lax.rem(slot, 2)
        source = blk_of(
            lax.rem(yi + offset_at(place, ny), ny), zi, core + other - 2 * core * other
        )
        for page in range(per_slot):
            node = node_s[source * per_slot + page]
            used = fill_s[source * per_slot + page]
            node = jnp.full((page_len, LANES), node, I32)
            leaf = node - 1 - MIDS
            is_mid = (node >= 1) & (leaf < 0)
            is_leaf = leaf >= 0
            bad = (
                (lane_page >= 0)
                & (lane_page < MIDS)
                & ((slot_at >= used) | (is_mid & (lane_page != node - 1)))
            )
            bad = bad | (
                is_leaf
                & (lane_page >= MIDS)
                & (lane_page < 2 * MIDS)
                & (lane_page - MIDS != lax.shift_right_arithmetic(leaf, 3))
            )
            bad = bad | (
                is_leaf
                & (lane_page >= 2 * MIDS)
                & (lane_page < 3 * MIDS)
                & (lane_page - 2 * MIDS != (leaf & 7))
            )
            at = pl.multiple_of((slot * per_slot + page) * page_len, page_len)
            keys[pl.ds(at, page_len), :] = jnp.where(bad, NEGATIVE, 0.0).astype(BF16)

    vals[HD:, :] = jnp.ones((vals.shape[0] - HD, vals.shape[1]), BF16)
    low_one = jnp.where(low[:1], 1.0, 0.0).astype(BF16)

    def build_queries(place):
        for half in range(heads // 2):
            two = qbuf[place, :, half * LANES : (half + 1) * LANES]
            turned = pltpu.roll(two.astype(F32), HD, 1).astype(BF16)
            extra = hot[place]
            base = 2 * half * rows
            qaug[place, base : base + rows, :] = two * low_one + extra
            qaug[place, base + rows : base + 2 * rows, :] = turned * low_one + extra

    slot_keys = per_slot * page_len

    def build_keys(place):
        span = slice(2 * place * slot_keys, 2 * (place + 1) * slot_keys)
        both = kvb[2 * place : 2 * place + 2].reshape(2 * slot_keys, LANES)
        keys[span, :] = both * low_one + keys[span, :]
        vals[0:HD, span] = both.astype(F32).T[HD:].astype(BF16)

    def fold(scores, value):
        top = jnp.max(scores, axis=0, keepdims=True)
        weights = jnp.exp(scores - top).astype(BF16)
        return top, jnp.dot(value, weights, preferred_element_type=F32)

    pass_pages(3)
    half_places = ny // 2
    build_queries(0)

    copies[12].wait()
    for place in range(half_places):
        forward(place).wait_recv()
        build_keys(place)
    span_keys = 2 * half_places * slot_keys
    tile = 512 if span_keys % 512 == 0 else 384
    tiles = range(0, span_keys, tile)

    def item(index):
        half = lax.div(index, nz)
        at = lax.rem(index, nz)
        place = half * (nz - 1 - at) + (1 - half) * at
        return place, pl.multiple_of(half * span_keys, LANES)

    def score(index, into, at, top):
        place, first = item(index)
        found = lax.dot_general(
            keys[pl.ds(first + at, tile), :],
            qaug[place],
            (((1,), (1,)), ((), ())),
            preferred_element_type=F32,
        )
        into[pl.ds(at, tile), :] = found
        best = jnp.max(found.reshape(tile // 8, 8, group), axis=0)
        return best if top is None else jnp.maximum(top, best)

    def step_item(index, held, following, into, top):
        place, first = item(index)
        best = total = None
        for at in tiles:
            best = score(following, into, at, best)
            weights = jnp.exp(held[pl.ds(at, tile), :] - top).astype(BF16)
            more = jnp.dot(
                vals[:, pl.ds(first + at, tile)], weights, preferred_element_type=F32
            )
            total = more if total is None else total + more
        old_top = state_top[place]
        new_top = jnp.maximum(top, old_top)
        total = total * jnp.exp(top - new_top) + state_sum[place] * jnp.exp(old_top - new_top)
        state_sum[place] = total
        state_top[place] = new_top
        return jnp.max(best, axis=0, keepdims=True)

    def finish(index):
        place, _ = item(index)

        @pl.when((index >= nz) & (place > 0))
        def _():
            total = state_sum[place]
            if not O_RING:
                mass = total[HD : HD + 1]
                part[place] = (total[0:HD] * (1.0 / mass)).astype(BF16)
                part_lse[place] = state_top[place] + jnp.log(mass)
                for copy in part_copies(place):
                    copy.start()
                return

            @pl.when(place + 2 < nz)
            def _():
                for copy in part_copies(place + 2):
                    copy.wait_recv()

            own_top = state_top[place]
            far_top = got_lse[place + 2]
            top = jnp.maximum(own_top, far_top)
            own_scale = jnp.exp(own_top - top)
            far_scale = jnp.exp(far_top - top)
            mass = total[HD : HD + 1] * own_scale + far_scale
            share = 1.0 / mass
            result = total[0:HD] * (own_scale * share)
            result = result + got[place + 2].astype(F32) * (far_scale * share)
            part[place] = result.astype(BF16)
            part_lse[place] = top + jnp.log(mass)
            for copy in part_copies(place):
                copy.start()

    state_top[...] = jnp.full(state_top.shape, LOWEST, F32)
    state_sum[...] = jnp.zeros(state_sum.shape, F32)
    for place in (nz, nz + 1):
        got_lse[place] = jnp.full((1, group), NEGATIVE, F32)
        got[place] = jnp.zeros((HD, group), BF16)
    items = 2 * nz

    def two_items(turn, top):
        for hops in range(4, ny // 2 + 1):

            @pl.when(turn == hops - 3)
            def _():
                pass_pages(hops)

        for ahead in (1, 2):
            place = 2 * turn + ahead

            @pl.when(place < nz)
            def _():
                q_copy(place if Q_RING else mirror(place, nz)).wait_recv()
                if Q_RING:

                    @pl.when(place + 2 < nz)
                    def _():
                        q_copy(place + 2).start()

                build_queries(place)

            @pl.when(place == nz)
            def _():
                for line in range(half_places, ny):
                    forward(line).wait_recv()
                    build_keys(line)

        index = 2 * turn
        top = step_item(index, scores_a, index + 1, scores_b, top)
        finish(index)
        top = step_item(index + 1, scores_b, jnp.minimum(index + 2, items - 1), scores_a, top)
        finish(index + 1)
        return top

    best = None
    for at in tiles:
        best = score(0, scores_a, at, best)
    lax.fori_loop(0, nz, two_items, jnp.max(best, axis=0, keepdims=True))

    for step in range(1, 5):
        near_copy(step).wait_recv()
    near_rows = 5 * rows
    near_all = near[...].reshape(near_rows, LANES)
    near_scores = lax.dot_general(
        near_all * low_one, qaug[0], (((1,), (1,)), ((), ())), preferred_element_type=F32
    )
    start_lane = jnp.sum(
        jnp.where(
            iota((rows, group), 0) == lax.rem(iota((rows, group), 1), rows), own_start, 0
        ),
        axis=0,
        keepdims=True,
    )
    key_place = (blk - 4) * rows + iota((near_rows, group), 0)
    row_place = blk * rows + lax.rem(iota((near_rows, group), 1), rows)
    allowed = (key_place >= start_lane) & (key_place <= row_place)
    near_scores = jnp.where(allowed, near_scores, NEGATIVE)
    near_values = jnp.concatenate(
        [near_all.astype(F32).T[HD:].astype(BF16), jnp.ones((16, near_rows), BF16)], axis=0
    )
    near_top, near_sum = fold(near_scores, near_values)
    near_total = near_sum[HD : HD + 1]
    near_out = near_sum[0:HD] / near_total
    near_lse = near_top + jnp.log(near_total)

    own_sum = state_sum[0]
    own_total = own_sum[HD : HD + 1]
    lses = [near_lse, state_top[0] + jnp.log(own_total)]
    for place in (1, 2) if O_RING else range(1, nz):
        if place < nz:
            for copy in part_copies(place if O_RING else mirror(place, nz)):
                copy.wait_recv()
            lses.append(got_lse[place])
    top = functools.reduce(jnp.maximum, lses)
    shares = [jnp.exp(lse - top) for lse in lses]
    scale = 1.0 / functools.reduce(jnp.add, shares)
    joined = near_out * (shares[0] * scale)
    joined = joined + own_sum[0:HD] * (shares[1] * scale / own_total)
    for place in range(1, len(lses) - 1):
        joined = joined + got[place].astype(F32) * (shares[place + 1] * scale)
    for half in range(heads // 2):
        two = joined[:, half * LANES : (half + 1) * LANES]
        square = jnp.concatenate([two, pltpu.roll(two, rows, 1)], axis=0)
        att[hx, :, half * LANES : (half + 1) * LANES] = square.T[0:rows].astype(BF16)
    for step in range(1, nx):
        att_copy(step).start()

    copies[13].wait()
    total = jnp.dot(att[hx], wob[hx], preferred_element_type=F32)
    for step in range(1, nx):
        wo_copy(step).wait_recv()
        att_copy(step).wait_recv()
        source = lax.rem(hx + nx - step, nx)
        total = total + jnp.dot(att[source], wob[source], preferred_element_type=F32)
    out[...] = total.astype(BF16)

    for place in range(1, ny):
        kv_copy(place).wait_send()
    for place in range(ny):
        forward(place).wait_send()
    for place in range(1, nz):
        q_copy(place).wait_send()
        for copy in part_copies(place):
            copy.wait_send()
    for step in range(1, 5):
        near_copy(step).wait_send()
    for step in range(1, nx):
        wo_copy(step).wait_send()
        att_copy(step).wait_send()


def local(
    tokens, q_weight, k_weight, v_weight, o_weight, kv_pages, page_node, page_fill, req_len, req_leaf, leaf_parent
):
    nx = lax.axis_size("head")
    ny, nz = LINES[lax.axis_size("blk")]
    rows, width = tokens.shape
    heads = q_weight.shape[1] // HD
    group = heads * rows
    out_cols = o_weight.shape[1] // nx
    per_slot, page_len = kv_pages.shape[1:3]
    slots = 2 * ny
    all_keys = slots * per_slot * page_len
    pages = page_node.shape[0]
    reqs = req_len.shape[0]
    leaves = leaf_parent.shape[0]
    half = HD // 2
    freq = np.tile(ROPE_BASE ** (-np.arange(half) / half), LANES // half)[None, :]
    dma = pltpu.SemaphoreType.DMA
    scratch = [
        pltpu.VMEM((rows, width), BF16),
        pltpu.VMEM((width, heads * HD), BF16),
        pltpu.VMEM((2 * HD, width), BF16),
        pltpu.SMEM((pages,), I32),
        pltpu.SMEM((pages,), I32),
        pltpu.VMEM((1, pages), I32),
        pltpu.VMEM((1, pages), I32),
        pltpu.VMEM((1, reqs), I32),
        pltpu.VMEM((1, reqs), I32),
        pltpu.VMEM((1, leaves), I32),
        pltpu.VMEM((1, LANES), F32),
        pltpu.VMEM((slots, per_slot, page_len, LANES), BF16),
        pltpu.VMEM((all_keys, LANES), BF16),
        pltpu.VMEM((HD + 16, all_keys), BF16),
        pltpu.VMEM((5, rows, LANES), BF16),
        pltpu.VMEM((nz, rows, heads * HD), BF16),
        pltpu.VMEM((nz, rows, LANES), BF16),
        pltpu.VMEM((nz, group, LANES), BF16),
        pltpu.VMEM((nz, 1, group), F32),
        pltpu.VMEM((nz, HD + 16, group), F32),
        pltpu.VMEM((nz, HD, group), BF16),
        pltpu.VMEM((nz, 1, group), F32),
        pltpu.VMEM((nz + 2, HD, group), BF16),
        pltpu.VMEM((nz + 2, 1, group), F32),
        pltpu.VMEM((all_keys // 2, group), F32),
        pltpu.VMEM((all_keys // 2, group), F32),
        pltpu.VMEM((nx, rows, heads * HD), BF16),
        pltpu.VMEM((nx, heads * HD, out_cols), BF16),
        dma((14,)),
        dma((ny,)),
        dma((ny,)),
        dma((ny,)),
        dma((ny,)),
        dma((nz,)),
        dma((nz,)),
        dma((5,)),
        dma((5,)),
        dma((nz,)),
        dma((nz,)),
        dma((nz,)),
        dma((nz,)),
        dma((nx,)),
        dma((nx,)),
        dma((nx,)),
        dma((nx,)),
    ]
    anywhere = pl.BlockSpec(memory_space=pl.ANY)
    return pl.pallas_call(
        functools.partial(kernel, (nx, ny, nz, rows, heads)),
        out_shape=jax.ShapeDtypeStruct((rows, out_cols), BF16),
        in_specs=[anywhere] * 12,
        out_specs=pl.BlockSpec(memory_space=pltpu.VMEM),
        scratch_shapes=scratch,
        compiler_params=pltpu.CompilerParams(
            collective_id=0, has_side_effects=True, vmem_limit_bytes=56 << 20
        ),
        name="tree_attention",
    )(
        tokens,
        q_weight,
        k_weight.T,
        v_weight.T,
        o_weight,
        kv_pages,
        page_node,
        page_fill,
        req_len,
        req_leaf,
        leaf_parent,
        jnp.asarray(freq, F32),
    )


def solution(mesh):
    return jax.shard_map(
        local,
        mesh=mesh,
        in_specs=(
            P("blk", None),
            P(None, "head"),
            P(None, "head"),
            P(None, "head"),
            P("head", None),
            P("head", "blk", None, None),
            P(),
            P(),
            P(),
            P(),
            P(),
        ),
        out_specs=P("blk", "head"),
        check_vma=False,
    )
```

```python
import functools

import jax
import jax.numpy as jnp
import numpy as np
from jax import lax
from jax.experimental import pallas as pl
from jax.experimental.pallas import tpu as pltpu
from jax.sharding import PartitionSpec as P

HD = 64
MIDS = 8
LANES = 128
LINES = {128: (8, 8), 8: (2, 2)}
NEGATIVE = -1e30
LOWEST = -3e38
EPSILON = 1e-06
ROPE_BASE = 10000.0
SCORE_SCALE = 0.125
MESH = pl.DeviceIdType.MESH
F32 = jnp.float32
BF16 = jnp.bfloat16
I32 = jnp.int32


def offset_at(place, count):
    if isinstance(place, int):
        half = (place + 1) // 2
        return half if place % 2 else (count - half) % count
    half = lax.div(place + 1, 2)
    odd = lax.rem(place, 2)
    return lax.rem(odd * half + (1 - odd) * (count - half), count)


def mirror(place, count):
    if isinstance(place, int):
        if place in (0, count - 1):
            return place
        return place + 1 if place % 2 else place - 1
    odd = lax.rem(place, 2)
    ends = jnp.logical_or(place == 0, place == count - 1)
    return jnp.where(ends, place, place + 2 * odd - 1)


def iota(shape, axis):
    return lax.broadcasted_iota(I32, shape, axis)


def kernel(
    sizes,
    tok,
    wq,
    wk,
    wv,
    wo,
    pages,
    node_hbm,
    fill_hbm,
    len_hbm,
    leaf_hbm,
    parent_hbm,
    freq_hbm,
    att,
    wob,
    tok_v,
    wq_v,
    wkv_v,
    node_s,
    fill_s,
    node_v,
    fill_v,
    len_v,
    leaf_v,
    parent_v,
    freq_v,
    kvb,
    keys,
    vals,
    near,
    qbuf,
    hot,
    qaug,
    state_top,
    state_sum,
    part,
    part_lse,
    got,
    got_lse,
    scores_a,
    scores_b,
    own_att,
    loc,
    kv_ss,
    kv_rs,
    fw_ss,
    fw_rs,
    q_ss,
    q_rs,
    nr_ss,
    nr_rs,
    o_ss,
    o_rs,
    l_ss,
    l_rs,
    w_ss,
    w_rs,
    a_ss,
    a_rs,
):
    nx, ny, nz, rows, heads = sizes
    group = heads * rows
    out_cols = wob.shape[1]
    width = heads * HD
    n_blk = ny * nz * 2
    hx = lax.axis_index("head")
    blk = lax.axis_index("blk")
    core = lax.rem(blk, 2)
    zi = lax.rem(lax.div(blk, 2), nz)
    yi = lax.div(blk, 2 * nz)

    def blk_of(y, z, c):
        return (y * nz + z) * 2 + c

    def y_peer(place):
        return blk_of(lax.rem(yi + offset_at(place, ny), ny), zi, core)

    def z_peer(place):
        return blk_of(yi, lax.rem(zi + offset_at(place, nz), nz), core)

    sibling = blk_of(yi, zi, 1 - core)

    my_rows = pl.ds(pl.multiple_of(hx * width, LANES), width)
    copies = [
        pltpu.make_async_copy(src, dst, loc.at[at])
        for at, (src, dst) in enumerate(
            [
                (len_hbm, len_v.at[0]),
                (leaf_hbm, leaf_v.at[0]),
                (parent_hbm, parent_v.at[0]),
                (node_hbm, node_v.at[0]),
                (fill_hbm, fill_v.at[0]),
                (freq_hbm, freq_v),
                (node_hbm, node_s),
                (fill_hbm, fill_s),
                (tok, tok_v),
                (wq, wq_v),
                (wk, wkv_v.at[0:HD]),
                (wv, wkv_v.at[HD:]),
                (pages.at[0], kvb.at[0]),
                (wo.at[:, pl.ds(pl.multiple_of(hx * out_cols, LANES), out_cols)], wob.at[my_rows]),
            ]
        )
    ]
    for at in (8, 9, 10, 11, 0, 1, 2, 3, 4, 5, 6, 7, 12):
        copies[at].start()

    barrier = pltpu.get_barrier_semaphore()
    greeted = []
    for place in range(max(ny, nz) - 1, 0, -1):
        greeted += [y_peer(place)] if place < ny else []
        greeted += [z_peer(place)] if place < nz else []
    greeted.append(sibling)
    for step in range(1, 5):
        if step < n_blk:
            greeted += [lax.rem(blk + step, n_blk), lax.rem(blk + n_blk - step, n_blk)]
    for peer in greeted:
        pl.semaphore_signal(barrier, inc=1, device_id=(hx, peer), device_id_type=MESH)
    for step in range(1, nx):
        pl.semaphore_signal(
            barrier, inc=1, device_id=(lax.rem(hx + step, nx), blk), device_id_type=MESH
        )

    def remote(src, dst, send, recv, to_head, to_blk):
        return pltpu.make_async_remote_copy(
            src_ref=src,
            dst_ref=dst,
            send_sem=send,
            recv_sem=recv,
            device_id=(to_head, to_blk),
            device_id_type=MESH,
        )

    def kv_copy(place):
        back = mirror(place, ny)
        return remote(
            pages.at[0], kvb.at[back], kv_ss.at[place], kv_rs.at[back], hx, y_peer(place)
        )

    def forward(place):
        src = kvb.at[place] if place else pages.at[0]
        return remote(src, kvb.at[ny + place], fw_ss.at[place], fw_rs.at[place], hx, sibling)

    def pass_pages(place):
        kv_copy(mirror(place, ny)).wait_recv()
        forward(place).start()

    def wo_copy(step):
        to = lax.rem(hx + step, nx)
        cols = pl.ds(pl.multiple_of(to * out_cols, LANES), out_cols)
        return remote(wo.at[:, cols], wob.at[my_rows], w_ss.at[step], w_rs.at[step], to, blk)

    def near_copy(step):
        to = lax.rem(blk + step, n_blk)
        return remote(near.at[4], near.at[4 - step], nr_ss.at[step], nr_rs.at[step], hx, to)

    def q_copy(place):
        back = mirror(place, nz)
        return remote(
            qbuf.at[0], qbuf.at[back], q_ss.at[place], q_rs.at[back], hx, z_peer(place)
        )

    def part_copies(place):
        back = mirror(place, nz)
        to = z_peer(place)
        return (
            remote(part.at[place], got.at[back], o_ss.at[place], o_rs.at[back], hx, to),
            remote(part_lse.at[place], got_lse.at[back], l_ss.at[place], l_rs.at[back], hx, to),
        )

    def att_copy(step):
        to = lax.rem(hx + step, nx)
        return remote(own_att, att.at[:, my_rows], a_ss.at[step], a_rs.at[step], to, blk)

    pl.semaphore_wait(barrier, len(greeted) + nx - 1)
    half_places = ny // 2
    for place in range(1, half_places):
        kv_copy(mirror(place, ny)).start()
    forward(0).start()

    for copy in copies[:6]:
        copy.wait()
    reqs = len_v.shape[1]
    leaves = parent_v.shape[1]
    diag = iota((reqs, reqs), 0) == iota((reqs, reqs), 1)

    def to_column(row):
        return jnp.sum(jnp.where(diag, row, 0), axis=1, keepdims=True)

    def to_row(column):
        return jnp.sum(jnp.where(diag, column, 0), axis=0, keepdims=True)

    len_row = len_v[...]
    len_col = to_column(len_row)
    upto = iota((reqs, reqs), 0) <= iota((reqs, reqs), 1)
    end_row = jnp.sum(jnp.where(upto, len_col, 0), axis=0, keepdims=True)
    start_row = end_row - len_row
    leaf_col = to_column(leaf_v[...])
    leaf_hit = leaf_col == iota((reqs, leaves), 1)
    mid_col = jnp.sum(jnp.where(leaf_hit, parent_v[...], 0), axis=1, keepdims=True)
    node_row = node_v[...]
    on_path = (node_row == 0) | (node_row == 1 + mid_col) | (node_row == 1 + MIDS + leaf_col)
    prefix_col = jnp.sum(jnp.where(on_path, fill_v[...], 0), axis=1, keepdims=True)
    shift_row = to_row(prefix_col) - start_row
    lane_req = iota((reqs, LANES), 1) - HD
    path_hot = (
        (lane_req == mid_col)
        & (lane_req < MIDS)
        | (lane_req - MIDS == lax.shift_right_logical(leaf_col, 3)) & (lane_req < 2 * MIDS)
        | (lane_req - 2 * MIDS == (leaf_col & 7)) & (lane_req < 3 * MIDS)
    ) & (lane_req >= 0)
    path_table = jnp.where(path_hot, 1.0, 0.0).astype(BF16)

    def requests_of(device):
        place = device * rows + iota((rows, reqs), 0)
        return (place >= start_row) & (place < end_row)

    own_hit = requests_of(blk)
    own_place = blk * rows + iota((rows, 1), 0)
    own_start = jnp.sum(jnp.where(own_hit, start_row, 0), axis=1, keepdims=True)
    position = own_place + jnp.sum(jnp.where(own_hit, shift_row, 0), axis=1, keepdims=True)
    angles = position.astype(F32) * freq_v[...]
    cosine = jnp.cos(angles)
    sine = jnp.sin(angles)
    lane = iota((rows, LANES), 1)
    first_half = lax.rem(lane, HD) < HD // 2
    sine = jnp.where(first_half, -sine, sine)
    low = lane < HD

    def rotated(v, cos, sin):
        swapped = jnp.where(
            first_half,
            pltpu.roll(v, LANES - HD // 2, 1),
            pltpu.roll(v, HD // 2, 1),
        )
        return v * cos + swapped * sin

    copies[8].wait()
    wide = tok_v[...].astype(F32)
    normed = (wide * lax.rsqrt(jnp.mean(wide * wide, axis=1, keepdims=True) + EPSILON)).astype(BF16)
    copies[9].wait()
    queries = jnp.dot(normed, wq_v[...], preferred_element_type=F32)
    for half in range(heads // 2):
        turned = rotated(queries[:, half * LANES : (half + 1) * LANES], cosine, sine)
        qbuf[0, :, half * LANES : (half + 1) * LANES] = turned.astype(BF16) * SCORE_SCALE
    for place in range(1, nz):
        q_copy(place).start()
    for place in range(half_places, ny):
        kv_copy(mirror(place, ny)).start()
    copies[10].wait()
    copies[11].wait()
    pack = lax.dot_general(
        normed, wkv_v[...], (((1,), (1,)), ((), ())), preferred_element_type=F32
    )
    pack = rotated(pack, jnp.where(low, cosine, 1.0), jnp.where(low, sine, 0.0))
    near[4] = pack.astype(BF16)
    for step in range(1, 5):
        near_copy(step).start()
    copies[13].start()
    for step in range(1, nx):
        wo_copy(step).start()

    @pl.loop(0, nz)
    def _(place):
        hit = jnp.where(requests_of(z_peer(place)), 1.0, 0.0).astype(BF16)
        hot[place] = jnp.dot(hit, path_table, preferred_element_type=F32).astype(BF16)

    copies[6].wait()
    copies[7].wait()
    page_len = pages.shape[2]
    per_slot = pages.shape[1]
    lane_page = iota((page_len, LANES), 1) - HD
    slot_at = iota((page_len, LANES), 0)

    @pl.loop(0, 2 * ny)
    def _(slot):
        place = lax.rem(slot, ny)
        other = lax.div(slot, ny)
        pair = lax.div(slot, 2)
        turned = jnp.where(pair == ny // 2 - 1, 1, jnp.where(pair == ny // 2, -1, 0))
        spot = slot + 2 * turned
        source = blk_of(
            lax.rem(yi + offset_at(place, ny), ny), zi, core + other - 2 * core * other
        )
        for page in range(per_slot):
            node = node_s[source * per_slot + page]
            used = fill_s[source * per_slot + page]
            node = jnp.full((page_len, LANES), node, I32)
            leaf = node - 1 - MIDS
            is_mid = (node >= 1) & (leaf < 0)
            is_leaf = leaf >= 0
            bad = (
                (lane_page >= 0)
                & (lane_page < MIDS)
                & ((slot_at >= used) | (is_mid & (lane_page != node - 1)))
            )
            bad = bad | (
                is_leaf
                & (lane_page >= MIDS)
                & (lane_page < 2 * MIDS)
                & (lane_page - MIDS != lax.shift_right_arithmetic(leaf, 3))
            )
            bad = bad | (
                is_leaf
                & (lane_page >= 2 * MIDS)
                & (lane_page < 3 * MIDS)
                & (lane_page - 2 * MIDS != (leaf & 7))
            )
            at = pl.multiple_of((spot * per_slot + page) * page_len, page_len)
            keys[pl.ds(at, page_len), :] = jnp.where(bad, NEGATIVE, 0.0).astype(BF16)

    vals[HD:, :] = jnp.ones((vals.shape[0] - HD, vals.shape[1]), BF16)
    low_one = jnp.where(low[:1], 1.0, 0.0).astype(BF16)

    def build_queries(place):
        for half in range(heads // 2):
            two = qbuf[place, :, half * LANES : (half + 1) * LANES]
            turned = pltpu.roll(two.astype(F32), HD, 1).astype(BF16)
            extra = hot[place]
            base = 2 * half * rows
            qaug[place, base : base + rows, :] = two * low_one + extra
            qaug[place, base + rows : base + 2 * rows, :] = turned * low_one + extra

    slot_keys = per_slot * page_len

    def build_keys(pair):
        spot = {ny // 2 - 1: ny // 2, ny // 2: ny // 2 - 1}.get(pair, pair)
        span = slice(2 * spot * slot_keys, 2 * (spot + 1) * slot_keys)
        both = kvb[2 * pair : 2 * pair + 2].reshape(2 * slot_keys, LANES)
        keys[span, :] = both * low_one + keys[span, :]
        vals[0:HD, span] = both.astype(F32).T[HD:].astype(BF16)

    def fold(scores, value):
        top = jnp.max(scores, axis=0, keepdims=True)
        weights = jnp.exp(scores - top).astype(BF16)
        return top, jnp.dot(value, weights, preferred_element_type=F32)

    build_queries(0)
    for place in range(1, ny - 2):
        pass_pages(place)

    copies[12].wait()
    for pair in range(half_places - 1):
        build_keys(pair)
    for place in (0, 1):
        if place < ny - 2:
            forward(place).wait_recv()
        elif place < ny:
            pass_pages(place) if place else None
            forward(place).wait_recv()
    build_keys(half_places)
    span_keys = 2 * half_places * slot_keys
    tile = 512 if span_keys % 512 == 0 else 384
    tiles = range(0, span_keys, tile)

    def item(index):
        half = lax.div(index, nz)
        at = lax.rem(index, nz)
        place = half * (nz - 1 - at) + (1 - half) * at
        return place, pl.multiple_of(half * span_keys, LANES)

    def score(index, into, at, top):
        place, first = item(index)
        found = lax.dot_general(
            keys[pl.ds(first + at, tile), :],
            qaug[place],
            (((1,), (1,)), ((), ())),
            preferred_element_type=F32,
        )
        into[pl.ds(at, tile), :] = found
        best = jnp.max(found.reshape(tile // 8, 8, group), axis=0)
        return best if top is None else jnp.maximum(top, best)

    def step_item(index, held, following, into, top):
        place, first = item(index)
        best = total = None
        for at in tiles:
            best = score(following, into, at, best)
            weights = jnp.exp(held[pl.ds(at, tile), :] - top).astype(BF16)
            more = jnp.dot(
                vals[:, pl.ds(first + at, tile)], weights, preferred_element_type=F32
            )
            total = more if total is None else total + more
        old_top = state_top[place]
        new_top = jnp.maximum(top, old_top)
        total = total * jnp.exp(top - new_top) + state_sum[place] * jnp.exp(old_top - new_top)
        state_sum[place] = total
        state_top[place] = new_top
        return jnp.max(best, axis=0, keepdims=True)

    def finish(index):
        place, _ = item(index)

        @pl.when((index >= nz) & (place > 0))
        def _():
            total = state_sum[place]
            mass = total[HD : HD + 1]
            part[place] = (total[0:HD] * (1.0 / mass)).astype(BF16)
            part_lse[place] = state_top[place] + jnp.log(mass)
            for copy in part_copies(place):
                copy.start()

    state_top[...] = jnp.full(state_top.shape, LOWEST, F32)
    state_sum[...] = jnp.zeros(state_sum.shape, F32)
    items = 2 * nz

    def fetch(place):
        @pl.when(place < nz)
        def _():
            q_copy(mirror(place, nz)).wait_recv()
            build_queries(place)

    def two_items(turn, top):
        for line in range(max(2, ny - 2), ny):

            @pl.when(turn == max(0, nz // 2 - 2))
            def _():
                pass_pages(line)

        index = 2 * turn
        fetch(index + 1)
        top = step_item(index, scores_a, index + 1, scores_b, top)
        finish(index)
        fetch(index + 2)

        @pl.when(index + 2 == nz)
        def _():
            build_keys(half_places - 1)
            for line in range(2, ny):
                forward(line).wait_recv()
                if line % 2:
                    build_keys(half_places + line // 2)

        top = step_item(index + 1, scores_b, jnp.minimum(index + 2, items - 1), scores_a, top)
        finish(index + 1)
        return top

    best = None
    for at in tiles:
        best = score(0, scores_a, at, best)
    lax.fori_loop(0, nz, two_items, jnp.max(best, axis=0, keepdims=True))

    for step in range(1, 5):
        near_copy(step).wait_recv()
    near_rows = 5 * rows
    near_all = near[...].reshape(near_rows, LANES)
    near_scores = lax.dot_general(
        near_all * low_one, qaug[0], (((1,), (1,)), ((), ())), preferred_element_type=F32
    )
    start_lane = jnp.sum(
        jnp.where(
            iota((rows, group), 0) == lax.rem(iota((rows, group), 1), rows), own_start, 0
        ),
        axis=0,
        keepdims=True,
    )
    key_place = (blk - 4) * rows + iota((near_rows, group), 0)
    row_place = blk * rows + lax.rem(iota((near_rows, group), 1), rows)
    allowed = (key_place >= start_lane) & (key_place <= row_place)
    near_scores = jnp.where(allowed, near_scores, NEGATIVE)
    near_values = jnp.concatenate(
        [near_all.astype(F32).T[HD:].astype(BF16), jnp.ones((16, near_rows), BF16)], axis=0
    )
    near_top, near_sum = fold(near_scores, near_values)
    near_total = near_sum[HD : HD + 1]
    near_out = near_sum[0:HD] / near_total
    near_lse = near_top + jnp.log(near_total)

    own_sum = state_sum[0]
    own_total = own_sum[HD : HD + 1]
    lses = [near_lse, state_top[0] + jnp.log(own_total)]
    for place in range(1, nz):
        for copy in part_copies(mirror(place, nz)):
            copy.wait_recv()
        lses.append(got_lse[place])
    top = functools.reduce(jnp.maximum, lses)
    shares = [jnp.exp(lse - top) for lse in lses]
    scale = 1.0 / functools.reduce(jnp.add, shares)
    joined = near_out * (shares[0] * scale)
    joined = joined + own_sum[0:HD] * (shares[1] * scale / own_total)
    for place in range(1, len(lses) - 1):
        joined = joined + got[place].astype(F32) * (shares[place + 1] * scale)
    for half in range(heads // 2):
        two = joined[:, half * LANES : (half + 1) * LANES]
        square = jnp.concatenate([two, pltpu.roll(two, rows, 1)], axis=0)
        own_att[:, half * LANES : (half + 1) * LANES] = square.T[0:rows].astype(BF16)
    for step in range(1, nx):
        att_copy(step).start()

    own_copy = pltpu.make_async_copy(own_att, att.at[:, my_rows], loc.at[14])
    own_copy.start()
    copies[13].wait()
    own_copy.wait()
    for step in range(1, nx):
        wo_copy(step).wait_recv()
        att_copy(step).wait_recv()

    for place in range(1, ny):
        kv_copy(place).wait_send()
    for place in range(ny):
        forward(place).wait_send()
    for place in range(1, nz):
        q_copy(place).wait_send()
        for copy in part_copies(place):
            copy.wait_send()
    for step in range(1, 5):
        near_copy(step).wait_send()
    for step in range(1, nx):
        wo_copy(step).wait_send()
        att_copy(step).wait_send()


def local(
    tokens, q_weight, k_weight, v_weight, o_weight, kv_pages, page_node, page_fill, req_len, req_leaf, leaf_parent
):
    nx = lax.axis_size("head")
    ny, nz = LINES[lax.axis_size("blk")]
    rows, width = tokens.shape
    heads = q_weight.shape[1] // HD
    group = heads * rows
    out_cols = o_weight.shape[1] // nx
    per_slot, page_len = kv_pages.shape[1:3]
    slots = 2 * ny
    all_keys = slots * per_slot * page_len
    pages = page_node.shape[0]
    reqs = req_len.shape[0]
    leaves = leaf_parent.shape[0]
    half = HD // 2
    freq = np.tile(ROPE_BASE ** (-np.arange(half) / half), LANES // half)[None, :]
    dma = pltpu.SemaphoreType.DMA
    scratch = [
        pltpu.VMEM((rows, width), BF16),
        pltpu.VMEM((width, heads * HD), BF16),
        pltpu.VMEM((2 * HD, width), BF16),
        pltpu.SMEM((pages,), I32),
        pltpu.SMEM((pages,), I32),
        pltpu.VMEM((1, pages), I32),
        pltpu.VMEM((1, pages), I32),
        pltpu.VMEM((1, reqs), I32),
        pltpu.VMEM((1, reqs), I32),
        pltpu.VMEM((1, leaves), I32),
        pltpu.VMEM((1, LANES), F32),
        pltpu.VMEM((slots, per_slot, page_len, LANES), BF16),
        pltpu.VMEM((all_keys, LANES), BF16),
        pltpu.VMEM((HD + 16, all_keys), BF16),
        pltpu.VMEM((5, rows, LANES), BF16),
        pltpu.VMEM((nz, rows, heads * HD), BF16),
        pltpu.VMEM((nz, rows, LANES), BF16),
        pltpu.VMEM((nz, group, LANES), BF16),
        pltpu.VMEM((nz, 1, group), F32),
        pltpu.VMEM((nz, HD + 16, group), F32),
        pltpu.VMEM((nz, HD, group), BF16),
        pltpu.VMEM((nz, 1, group), F32),
        pltpu.VMEM((nz, HD, group), BF16),
        pltpu.VMEM((nz, 1, group), F32),
        pltpu.VMEM((all_keys // 2, group), F32),
        pltpu.VMEM((all_keys // 2, group), F32),
        pltpu.VMEM((rows, heads * HD), BF16),
        dma((15,)),
        dma((ny,)),
        dma((ny,)),
        dma((ny,)),
        dma((ny,)),
        dma((nz,)),
        dma((nz,)),
        dma((5,)),
        dma((5,)),
        dma((nz,)),
        dma((nz,)),
        dma((nz,)),
        dma((nz,)),
        dma((nx,)),
        dma((nx,)),
        dma((nx,)),
        dma((nx,)),
    ]
    anywhere = pl.BlockSpec(memory_space=pl.ANY)
    attended, columns = pl.pallas_call(
        functools.partial(kernel, (nx, ny, nz, rows, heads)),
        out_shape=[
            jax.ShapeDtypeStruct((rows, nx * heads * HD), BF16),
            jax.ShapeDtypeStruct((nx * heads * HD, out_cols), BF16),
        ],
        in_specs=[anywhere] * 12,
        out_specs=[anywhere, anywhere],
        scratch_shapes=scratch,
        compiler_params=pltpu.CompilerParams(
            collective_id=0, has_side_effects=True, vmem_limit_bytes=56 << 20
        ),
        name="tree_attention",
    )(
        tokens,
        q_weight,
        k_weight.T,
        v_weight.T,
        o_weight,
        kv_pages,
        page_node,
        page_fill,
        req_len,
        req_leaf,
        leaf_parent,
        jnp.asarray(freq, F32),
    )
    return jnp.dot(attended, columns, preferred_element_type=F32).astype(BF16)


def solution(mesh):
    return jax.shard_map(
        local,
        mesh=mesh,
        in_specs=(
            P("blk", None),
            P(None, "head"),
            P(None, "head"),
            P(None, "head"),
            P("head", None),
            P("head", "blk", None, None),
            P(),
            P(),
            P(),
            P(),
            P(),
        ),
        out_specs=P("blk", "head"),
        check_vma=False,
    )
```

```python
import functools

import jax
import jax.numpy as jnp
import numpy as np
from jax import lax
from jax.experimental import pallas as pl
from jax.experimental.pallas import tpu as pltpu
from jax.sharding import PartitionSpec as P

HD = 64
MIDS = 8
LANES = 128
LINES = {128: (8, 8), 8: (2, 2)}
NEGATIVE = -1e30
LOWEST = -3e38
EPSILON = 1e-06
ROPE_BASE = 10000.0
SCORE_SCALE = 0.125
MESH = pl.DeviceIdType.MESH
F32 = jnp.float32
BF16 = jnp.bfloat16
I32 = jnp.int32


def offset_at(place, count):
    if isinstance(place, int):
        half = (place + 1) // 2
        return half if place % 2 else (count - half) % count
    half = lax.div(place + 1, 2)
    odd = lax.rem(place, 2)
    return lax.rem(odd * half + (1 - odd) * (count - half), count)


def mirror(place, count):
    if isinstance(place, int):
        if place in (0, count - 1):
            return place
        return place + 1 if place % 2 else place - 1
    odd = lax.rem(place, 2)
    ends = jnp.logical_or(place == 0, place == count - 1)
    return jnp.where(ends, place, place + 2 * odd - 1)


def iota(shape, axis):
    return lax.broadcasted_iota(I32, shape, axis)


def kernel(
    sizes,
    tok,
    wq,
    wk,
    wv,
    wo,
    pages,
    node_hbm,
    fill_hbm,
    len_hbm,
    leaf_hbm,
    parent_hbm,
    freq_hbm,
    att,
    wob,
    tok_v,
    wq_v,
    wkv_v,
    node_s,
    fill_s,
    node_v,
    fill_v,
    len_v,
    leaf_v,
    parent_v,
    freq_v,
    kvb,
    keys,
    vals,
    near,
    qbuf,
    hot,
    qaug,
    state_top,
    state_sum,
    part,
    part_lse,
    got,
    got_lse,
    scores_a,
    scores_b,
    own_att,
    loc,
    kv_ss,
    kv_rs,
    fw_ss,
    fw_rs,
    q_ss,
    q_rs,
    nr_ss,
    nr_rs,
    o_ss,
    o_rs,
    l_ss,
    l_rs,
    w_ss,
    w_rs,
    a_ss,
    a_rs,
):
    nx, ny, nz, rows, heads = sizes
    group = heads * rows
    out_cols = wob.shape[1]
    width = heads * HD
    n_blk = ny * nz * 2
    hx = lax.axis_index("head")
    blk = lax.axis_index("blk")
    core = lax.rem(blk, 2)
    zi = lax.rem(lax.div(blk, 2), nz)
    yi = lax.div(blk, 2 * nz)

    def blk_of(y, z, c):
        return (y * nz + z) * 2 + c

    def y_peer(place):
        return blk_of(lax.rem(yi + offset_at(place, ny), ny), zi, core)

    def z_peer(place):
        return blk_of(yi, lax.rem(zi + offset_at(place, nz), nz), core)

    sibling = blk_of(yi, zi, 1 - core)

    my_rows = pl.ds(pl.multiple_of(hx * width, LANES), width)
    copies = [
        pltpu.make_async_copy(src, dst, loc.at[at])
        for at, (src, dst) in enumerate(
            [
                (len_hbm, len_v.at[0]),
                (leaf_hbm, leaf_v.at[0]),
                (parent_hbm, parent_v.at[0]),
                (node_hbm, node_v.at[0]),
                (fill_hbm, fill_v.at[0]),
                (freq_hbm, freq_v),
                (node_hbm, node_s),
                (fill_hbm, fill_s),
                (tok, tok_v),
                (wq, wq_v),
                (wk, wkv_v.at[0:HD]),
                (wv, wkv_v.at[HD:]),
                (pages.at[0], kvb.at[0]),
                (wo.at[:, pl.ds(pl.multiple_of(hx * out_cols, LANES), out_cols)], wob.at[my_rows]),
            ]
        )
    ]
    for at in (8, 9, 10, 11, 0, 1, 2, 3, 4, 5, 6, 7, 12):
        copies[at].start()

    barrier = pltpu.get_barrier_semaphore()
    greeted = []
    for place in range(max(ny, nz) - 1, 0, -1):
        greeted += [y_peer(place)] if place < ny else []
        greeted += [z_peer(place)] if place < nz else []
    greeted.append(sibling)
    for step in range(1, 5):
        if step < n_blk:
            greeted += [lax.rem(blk + step, n_blk), lax.rem(blk + n_blk - step, n_blk)]
    for peer in greeted:
        pl.semaphore_signal(barrier, inc=1, device_id=(hx, peer), device_id_type=MESH)
    for step in range(1, nx):
        pl.semaphore_signal(
            barrier, inc=1, device_id=(lax.rem(hx + step, nx), blk), device_id_type=MESH
        )

    def remote(src, dst, send, recv, to_head, to_blk):
        return pltpu.make_async_remote_copy(
            src_ref=src,
            dst_ref=dst,
            send_sem=send,
            recv_sem=recv,
            device_id=(to_head, to_blk),
            device_id_type=MESH,
        )

    def kv_copy(place):
        back = mirror(place, ny)
        return remote(
            pages.at[0], kvb.at[back], kv_ss.at[place], kv_rs.at[back], hx, y_peer(place)
        )

    def forward(place):
        src = kvb.at[place] if place else pages.at[0]
        return remote(src, kvb.at[ny + place], fw_ss.at[place], fw_rs.at[place], hx, sibling)

    def pass_pages(place):
        kv_copy(mirror(place, ny)).wait_recv()
        forward(place).start()

    def wo_copy(step):
        to = lax.rem(hx + step, nx)
        cols = pl.ds(pl.multiple_of(to * out_cols, LANES), out_cols)
        return remote(wo.at[:, cols], wob.at[my_rows], w_ss.at[step], w_rs.at[step], to, blk)

    def near_copy(step):
        to = lax.rem(blk + step, n_blk)
        return remote(near.at[4], near.at[4 - step], nr_ss.at[step], nr_rs.at[step], hx, to)

    def q_copy(place):
        back = mirror(place, nz)
        return remote(
            qbuf.at[0], qbuf.at[back], q_ss.at[place], q_rs.at[back], hx, z_peer(place)
        )

    def part_copies(place):
        back = mirror(place, nz)
        to = z_peer(place)
        return (
            remote(part.at[place], got.at[back], o_ss.at[place], o_rs.at[back], hx, to),
            remote(part_lse.at[place], got_lse.at[back], l_ss.at[place], l_rs.at[back], hx, to),
        )

    def att_copy(step):
        to = lax.rem(hx + step, nx)
        return remote(own_att, att.at[:, my_rows], a_ss.at[step], a_rs.at[step], to, blk)

    pl.semaphore_wait(barrier, len(greeted) + nx - 1)
    half_places = ny // 2
    for place in range(1, half_places):
        kv_copy(mirror(place, ny)).start()
    forward(0).start()

    for copy in copies[:6] + copies[8:12]:
        copy.wait()
    reqs = len_v.shape[1]
    leaves = parent_v.shape[1]
    diag = iota((reqs, reqs), 0) == iota((reqs, reqs), 1)

    def to_column(row):
        return jnp.sum(jnp.where(diag, row, 0), axis=1, keepdims=True)

    def to_row(column):
        return jnp.sum(jnp.where(diag, column, 0), axis=0, keepdims=True)

    len_row = len_v[...]
    len_col = to_column(len_row)
    upto = iota((reqs, reqs), 0) <= iota((reqs, reqs), 1)
    end_row = jnp.sum(jnp.where(upto, len_col, 0), axis=0, keepdims=True)
    start_row = end_row - len_row
    leaf_col = to_column(leaf_v[...])
    leaf_hit = leaf_col == iota((reqs, leaves), 1)
    mid_col = jnp.sum(jnp.where(leaf_hit, parent_v[...], 0), axis=1, keepdims=True)
    node_row = node_v[...]
    on_path = (node_row == 0) | (node_row == 1 + mid_col) | (node_row == 1 + MIDS + leaf_col)
    prefix_col = jnp.sum(jnp.where(on_path, fill_v[...], 0), axis=1, keepdims=True)
    shift_row = to_row(prefix_col) - start_row
    lane_req = iota((reqs, LANES), 1) - HD
    path_hot = (
        (lane_req == mid_col)
        & (lane_req < MIDS)
        | (lane_req - MIDS == lax.shift_right_logical(leaf_col, 3)) & (lane_req < 2 * MIDS)
        | (lane_req - 2 * MIDS == (leaf_col & 7)) & (lane_req < 3 * MIDS)
    ) & (lane_req >= 0)
    path_table = jnp.where(path_hot, 1.0, 0.0).astype(BF16)

    def requests_of(device):
        place = device * rows + iota((rows, reqs), 0)
        return (place >= start_row) & (place < end_row)

    own_hit = requests_of(blk)
    own_place = blk * rows + iota((rows, 1), 0)
    own_start = jnp.sum(jnp.where(own_hit, start_row, 0), axis=1, keepdims=True)
    position = own_place + jnp.sum(jnp.where(own_hit, shift_row, 0), axis=1, keepdims=True)
    angles = position.astype(F32) * freq_v[...]
    cosine = jnp.cos(angles)
    sine = jnp.sin(angles)
    lane = iota((rows, LANES), 1)
    first_half = lax.rem(lane, HD) < HD // 2
    sine = jnp.where(first_half, -sine, sine)
    low = lane < HD

    def rotated(v, cos, sin):
        swapped = jnp.where(
            first_half,
            pltpu.roll(v, LANES - HD // 2, 1),
            pltpu.roll(v, HD // 2, 1),
        )
        return v * cos + swapped * sin

    wide = tok_v[...].astype(F32)
    normed = (wide * lax.rsqrt(jnp.mean(wide * wide, axis=1, keepdims=True) + EPSILON)).astype(BF16)
    queries = jnp.dot(normed, wq_v[...], preferred_element_type=F32)
    for half in range(heads // 2):
        turned = rotated(queries[:, half * LANES : (half + 1) * LANES], cosine, sine)
        qbuf[0, :, half * LANES : (half + 1) * LANES] = turned.astype(BF16) * SCORE_SCALE
    for place in range(1, nz):
        q_copy(place).start()
    for place in range(half_places, ny):
        kv_copy(mirror(place, ny)).start()
    pack = lax.dot_general(
        normed, wkv_v[...], (((1,), (1,)), ((), ())), preferred_element_type=F32
    )
    pack = rotated(pack, jnp.where(low, cosine, 1.0), jnp.where(low, sine, 0.0))
    near[4] = pack.astype(BF16)
    for step in range(1, 5):
        near_copy(step).start()
    copies[13].start()
    for step in range(1, nx):
        wo_copy(step).start()

    @pl.loop(0, nz)
    def _(place):
        hit = jnp.where(requests_of(z_peer(place)), 1.0, 0.0).astype(BF16)
        hot[place] = jnp.dot(hit, path_table, preferred_element_type=F32).astype(BF16)

    copies[6].wait()
    copies[7].wait()
    page_len = pages.shape[2]
    per_slot = pages.shape[1]
    lane_page = iota((page_len, LANES), 1) - HD
    slot_at = iota((page_len, LANES), 0)

    @pl.loop(0, 2 * ny)
    def _(slot):
        place = lax.rem(slot, ny)
        other = lax.div(slot, ny)
        pair = lax.div(slot, 2)
        turned = jnp.where(pair == ny // 2 - 1, 1, jnp.where(pair == ny // 2, -1, 0))
        spot = slot + 2 * turned
        source = blk_of(
            lax.rem(yi + offset_at(place, ny), ny), zi, core + other - 2 * core * other
        )
        for page in range(per_slot):
            node = node_s[source * per_slot + page]
            used = fill_s[source * per_slot + page]
            node = jnp.full((page_len, LANES), node, I32)
            leaf = node - 1 - MIDS
            is_mid = (node >= 1) & (leaf < 0)
            is_leaf = leaf >= 0
            bad = (
                (lane_page >= 0)
                & (lane_page < MIDS)
                & ((slot_at >= used) | (is_mid & (lane_page != node - 1)))
            )
            bad = bad | (
                is_leaf
                & (lane_page >= MIDS)
                & (lane_page < 2 * MIDS)
                & (lane_page - MIDS != lax.shift_right_arithmetic(leaf, 3))
            )
            bad = bad | (
                is_leaf
                & (lane_page >= 2 * MIDS)
                & (lane_page < 3 * MIDS)
                & (lane_page - 2 * MIDS != (leaf & 7))
            )
            at = pl.multiple_of((spot * per_slot + page) * page_len, page_len)
            keys[pl.ds(at, page_len), :] = jnp.where(bad, NEGATIVE, 0.0).astype(BF16)

    vals[HD:, :] = jnp.ones((vals.shape[0] - HD, vals.shape[1]), BF16)
    low_one = jnp.where(low[:1], 1.0, 0.0).astype(BF16)

    def build_queries(place):
        for half in range(heads // 2):
            two = qbuf[place, :, half * LANES : (half + 1) * LANES]
            turned = pltpu.roll(two.astype(F32), HD, 1).astype(BF16)
            extra = hot[place]
            base = 2 * half * rows
            qaug[place, base : base + rows, :] = two * low_one + extra
            qaug[place, base + rows : base + 2 * rows, :] = turned * low_one + extra

    slot_keys = per_slot * page_len

    def build_keys(pair):
        spot = {ny // 2 - 1: ny // 2, ny // 2: ny // 2 - 1}.get(pair, pair)
        span = slice(2 * spot * slot_keys, 2 * (spot + 1) * slot_keys)
        both = kvb[2 * pair : 2 * pair + 2].reshape(2 * slot_keys, LANES)
        keys[span, :] = both * low_one + keys[span, :]
        vals[0:HD, span] = both.astype(F32).T[HD:].astype(BF16)

    def fold(scores, value):
        top = jnp.max(scores, axis=0, keepdims=True)
        weights = jnp.exp(scores - top).astype(BF16)
        return top, jnp.dot(value, weights, preferred_element_type=F32)

    build_queries(0)

    copies[12].wait()
    for place in range(1, ny - 2):
        pass_pages(place)
        if place % 2:
            build_keys(place // 2)
    for place in (0, 1):
        if place < ny - 2:
            forward(place).wait_recv()
        elif place < ny:
            pass_pages(place) if place else None
            forward(place).wait_recv()
    build_keys(half_places)
    span_keys = 2 * half_places * slot_keys
    tile = 512 if span_keys % 512 == 0 else 384
    tiles = range(0, span_keys, tile)

    def item(index):
        half = lax.div(index, nz)
        at = lax.rem(index, nz)
        place = half * (nz - 1 - at) + (1 - half) * at
        return place, pl.multiple_of(half * span_keys, LANES)

    def score(index, into, at, top):
        place, first = item(index)
        found = lax.dot_general(
            keys[pl.ds(first + at, tile), :],
            qaug[place],
            (((1,), (1,)), ((), ())),
            preferred_element_type=F32,
        )
        into[pl.ds(at, tile), :] = found
        best = jnp.max(found.reshape(tile // 8, 8, group), axis=0)
        return best if top is None else jnp.maximum(top, best)

    def step_item(index, held, following, into, top):
        place, first = item(index)
        best = total = None
        for at in tiles:
            best = score(following, into, at, best)
            weights = jnp.exp(held[pl.ds(at, tile), :] - top).astype(BF16)
            more = jnp.dot(
                vals[:, pl.ds(first + at, tile)], weights, preferred_element_type=F32
            )
            total = more if total is None else total + more
        old_top = state_top[place]
        new_top = jnp.maximum(top, old_top)
        total = total * jnp.exp(top - new_top) + state_sum[place] * jnp.exp(old_top - new_top)
        state_sum[place] = total
        state_top[place] = new_top
        return jnp.max(best, axis=0, keepdims=True)

    def finish(index):
        place, _ = item(index)

        @pl.when((index >= nz) & (place > 0))
        def _():
            total = state_sum[place]
            mass = total[HD : HD + 1]
            part[place] = (total[0:HD] * (1.0 / mass)).astype(BF16)
            part_lse[place] = state_top[place] + jnp.log(mass)
            for copy in part_copies(place):
                copy.start()

    state_top[...] = jnp.full(state_top.shape, LOWEST, F32)
    state_sum[...] = jnp.zeros(state_sum.shape, F32)
    items = 2 * nz

    def fetch(place):
        @pl.when(place < nz)
        def _():
            q_copy(mirror(place, nz)).wait_recv()
            build_queries(place)

    def two_items(turn, top):
        for line in range(max(2, ny - 2), ny):

            @pl.when(turn == max(0, nz // 2 - 2))
            def _():
                pass_pages(line)

        index = 2 * turn
        fetch(index + 1)
        top = step_item(index, scores_a, index + 1, scores_b, top)
        finish(index)
        fetch(index + 2)

        @pl.when(index + 2 == nz)
        def _():
            build_keys(half_places - 1)
            for line in range(2, ny):
                forward(line).wait_recv()
                if line % 2:
                    build_keys(half_places + line // 2)

        top = step_item(index + 1, scores_b, jnp.minimum(index + 2, items - 1), scores_a, top)
        finish(index + 1)
        return top

    best = None
    for at in tiles:
        best = score(0, scores_a, at, best)
    lax.fori_loop(0, nz, two_items, jnp.max(best, axis=0, keepdims=True))

    for step in range(1, 5):
        near_copy(step).wait_recv()
    near_rows = 5 * rows
    near_all = near[...].reshape(near_rows, LANES)
    near_scores = lax.dot_general(
        near_all * low_one, qaug[0], (((1,), (1,)), ((), ())), preferred_element_type=F32
    )
    start_lane = jnp.sum(
        jnp.where(
            iota((rows, group), 0) == lax.rem(iota((rows, group), 1), rows), own_start, 0
        ),
        axis=0,
        keepdims=True,
    )
    key_place = (blk - 4) * rows + iota((near_rows, group), 0)
    row_place = blk * rows + lax.rem(iota((near_rows, group), 1), rows)
    allowed = (key_place >= start_lane) & (key_place <= row_place)
    near_scores = jnp.where(allowed, near_scores, NEGATIVE)
    near_values = jnp.concatenate(
        [near_all.astype(F32).T[HD:].astype(BF16), jnp.ones((16, near_rows), BF16)], axis=0
    )
    near_top, near_sum = fold(near_scores, near_values)
    near_total = near_sum[HD : HD + 1]
    near_out = near_sum[0:HD] / near_total
    near_lse = near_top + jnp.log(near_total)

    own_sum = state_sum[0]
    own_total = own_sum[HD : HD + 1]
    lses = [near_lse, state_top[0] + jnp.log(own_total)]
    for place in range(1, nz):
        for copy in part_copies(mirror(place, nz)):
            copy.wait_recv()
        lses.append(got_lse[place])
    top = functools.reduce(jnp.maximum, lses)
    shares = [jnp.exp(lse - top) for lse in lses]
    scale = 1.0 / functools.reduce(jnp.add, shares)
    joined = near_out * (shares[0] * scale)
    joined = joined + own_sum[0:HD] * (shares[1] * scale / own_total)
    for place in range(1, len(lses) - 1):
        joined = joined + got[place].astype(F32) * (shares[place + 1] * scale)
    for half in range(heads // 2):
        two = joined[:, half * LANES : (half + 1) * LANES]
        square = jnp.concatenate([two, pltpu.roll(two, rows, 1)], axis=0)
        own_att[:, half * LANES : (half + 1) * LANES] = square.T[0:rows].astype(BF16)
    for step in range(1, nx):
        att_copy(step).start()

    own_copy = pltpu.make_async_copy(own_att, att.at[:, my_rows], loc.at[14])
    own_copy.start()
    copies[13].wait()
    own_copy.wait()
    for step in range(1, nx):
        wo_copy(step).wait_recv()
        att_copy(step).wait_recv()

    for place in range(1, ny):
        kv_copy(place).wait_send()
    for place in range(ny):
        forward(place).wait_send()
    for place in range(1, nz):
        q_copy(place).wait_send()
        for copy in part_copies(place):
            copy.wait_send()
    for step in range(1, 5):
        near_copy(step).wait_send()
    for step in range(1, nx):
        wo_copy(step).wait_send()
        att_copy(step).wait_send()


def product(attended, columns, out):
    out[...] = jnp.dot(attended[...], columns[...], preferred_element_type=F32).astype(BF16)


def local(
    tokens, q_weight, k_weight, v_weight, o_weight, kv_pages, page_node, page_fill, req_len, req_leaf, leaf_parent
):
    nx = lax.axis_size("head")
    ny, nz = LINES[lax.axis_size("blk")]
    rows, width = tokens.shape
    heads = q_weight.shape[1] // HD
    group = heads * rows
    out_cols = o_weight.shape[1] // nx
    per_slot, page_len = kv_pages.shape[1:3]
    slots = 2 * ny
    all_keys = slots * per_slot * page_len
    pages = page_node.shape[0]
    reqs = req_len.shape[0]
    leaves = leaf_parent.shape[0]
    half = HD // 2
    freq = np.tile(ROPE_BASE ** (-np.arange(half) / half), LANES // half)[None, :]
    dma = pltpu.SemaphoreType.DMA
    scratch = [
        pltpu.VMEM((rows, width), BF16),
        pltpu.VMEM((width, heads * HD), BF16),
        pltpu.VMEM((2 * HD, width), BF16),
        pltpu.SMEM((pages,), I32),
        pltpu.SMEM((pages,), I32),
        pltpu.VMEM((1, pages), I32),
        pltpu.VMEM((1, pages), I32),
        pltpu.VMEM((1, reqs), I32),
        pltpu.VMEM((1, reqs), I32),
        pltpu.VMEM((1, leaves), I32),
        pltpu.VMEM((1, LANES), F32),
        pltpu.VMEM((slots, per_slot, page_len, LANES), BF16),
        pltpu.VMEM((all_keys, LANES), BF16),
        pltpu.VMEM((HD + 16, all_keys), BF16),
        pltpu.VMEM((5, rows, LANES), BF16),
        pltpu.VMEM((nz, rows, heads * HD), BF16),
        pltpu.VMEM((nz, rows, LANES), BF16),
        pltpu.VMEM((nz, group, LANES), BF16),
        pltpu.VMEM((nz, 1, group), F32),
        pltpu.VMEM((nz, HD + 16, group), F32),
        pltpu.VMEM((nz, HD, group), BF16),
        pltpu.VMEM((nz, 1, group), F32),
        pltpu.VMEM((nz, HD, group), BF16),
        pltpu.VMEM((nz, 1, group), F32),
        pltpu.VMEM((all_keys // 2, group), F32),
        pltpu.VMEM((all_keys // 2, group), F32),
        pltpu.VMEM((rows, heads * HD), BF16),
        dma((15,)),
        dma((ny,)),
        dma((ny,)),
        dma((ny,)),
        dma((ny,)),
        dma((nz,)),
        dma((nz,)),
        dma((5,)),
        dma((5,)),
        dma((nz,)),
        dma((nz,)),
        dma((nz,)),
        dma((nz,)),
        dma((nx,)),
        dma((nx,)),
        dma((nx,)),
        dma((nx,)),
    ]
    anywhere = pl.BlockSpec(memory_space=pl.ANY)
    attended, columns = pl.pallas_call(
        functools.partial(kernel, (nx, ny, nz, rows, heads)),
        out_shape=[
            jax.ShapeDtypeStruct((rows, nx * heads * HD), BF16),
            jax.ShapeDtypeStruct((nx * heads * HD, out_cols), BF16),
        ],
        in_specs=[anywhere] * 12,
        out_specs=[anywhere, anywhere],
        scratch_shapes=scratch,
        compiler_params=pltpu.CompilerParams(
            collective_id=0, has_side_effects=True, vmem_limit_bytes=56 << 20
        ),
        name="tree_attention",
    )(
        tokens,
        q_weight,
        k_weight.T,
        v_weight.T,
        o_weight,
        kv_pages,
        page_node,
        page_fill,
        req_len,
        req_leaf,
        leaf_parent,
        jnp.asarray(freq, F32),
    )
    depth, steps = attended.shape[1], 2
    return pl.pallas_call(
        product,
        grid=(steps,),
        out_shape=jax.ShapeDtypeStruct((rows, out_cols), BF16),
        in_specs=[
            pl.BlockSpec((rows, depth), lambda at: (0, 0)),
            pl.BlockSpec((depth, out_cols // steps), lambda at: (0, at)),
        ],
        out_specs=pl.BlockSpec((rows, out_cols // steps), lambda at: (0, at)),
        compiler_params=pltpu.CompilerParams(vmem_limit_bytes=56 << 20),
        name="output_product",
    )(attended, columns)


def solution(mesh):
    return jax.shard_map(
        local,
        mesh=mesh,
        in_specs=(
            P("blk", None),
            P(None, "head"),
            P(None, "head"),
            P(None, "head"),
            P("head", None),
            P("head", "blk", None, None),
            P(),
            P(),
            P(),
            P(),
            P(),
        ),
        out_specs=P("blk", "head"),
        check_vma=False,
    )
```
